256 devices in a mesh: grp: 8 (over y, core), dev: 32 (over z, x).
Axes of the slice: x: 4, y: 4, z: 8, core: 2. Of those that a mesh axis runs over, the one named last changes fastest.
Arguments:
- objective: float32 [8, 32, 1024, 256], P('grp', 'dev'), may hold values from -24 to 24
- schur: float32 [8, 32, 1024, 1024], P('grp', 'dev')
- local_inverse: float32 [8, 32, 1024, 1024], P('grp', 'dev')
- coarse_basis: float32 [8, 32, 64, 1024], P('grp', 'dev'), may hold values from -0.09375 to 0.09375
- coarse_inverse: float32 [8, 32, 32, 8192], P(None, 'dev', None, 'grp')
- stiffness: int32 [8, 32, 1024], P('grp', 'dev'), may hold values from 1 to 8
- face_rows: int32 [8, 32, 4, 256], P('grp', 'dev'), may hold values from -1 to 1023, as said below
- coarse_map: int32 [8, 32, 64], P('grp', 'dev'), may hold values from 0 to 255
Outputs:
- adjoint: float32 [8, 32, 1024, 256], P('grp', 'dev')
The draws below stay inside these ranges and needn't reach their ends.
Inputs may be any that keep to these rules, and one draw needn't show every extreme that they name: `face_rows`: slot k of face p names the local row of the k-th row that the subdomain shares with its neighbour across face p, or -1; the live slots of a face come first, and the neighbour lists the same shared rows in the same order in its opposite face. The live slots of a subdomain name its rows 0 to n - 1 once each, n at most 1024, and at least one subdomain has all 1024 rows. Faces at the ends of the layout are empty; a face that joins two subdomains has 1 to 256 rows. `coarse_map`: entry e of subdomain (g, d) names the coarse dof (e // 32, d, e % 32), owned by the subdomain at grp index e // 32 of the same dev index.
All inputs are finite; a program needn't handle non-finite values.
Results may differ from the reference program's by a relative error of at most 0.0003.
Values sent between devices are 32-bit elements; how exact they have to be, the bound alone decides.
No kernel may reach another device: no remote copies, remote signals or barrier semaphores. Data moves between devices by JAX's collectives and lax.ppermute only.
A program may use at most 64 MiB of HBM per device.

```python
import math
import jax
import jax.numpy as jnp
from jax import lax

INTERFACE = 1024
FACE_ROWS = 256
COLUMNS = 256
OWNED = 32
COARSE_LOCAL = 64
SWEEPS = 2
COARSE = 8192
N_GRP = 8
N_DEV = 32


def dominant(key, order, low, high, spread):
    noise_key, diagonal_key = jax.random.split(key)
    shape = (N_GRP, N_DEV, order, order)
    off_part = jax.random.normal(noise_key, shape) * (spread / math.sqrt(order))
    diagonal = jax.random.uniform(diagonal_key, (N_GRP, N_DEV, order), minval=low, maxval=high)
    identity = jnp.eye(order, dtype=bool)
    return jnp.where(identity, off_part + diagonal[:, :, None, :], off_part)


def draw_schur(key, part):
    return dominant(jax.random.fold_in(key, 11), INTERFACE, 2.0, 4.0, 0.8)


def draw_local_inverse(key, part):
    return dominant(jax.random.fold_in(key, 23), INTERFACE, 0.12, 0.25, 0.05)


def draw_coarse_inverse(key, part):
    noise_key, diagonal_key = jax.random.split(jax.random.fold_in(key, 37))
    total = OWNED * N_GRP * N_DEV
    shape = (N_GRP, N_DEV, OWNED, total)
    off_part = jax.random.normal(noise_key, shape) * (0.5 / math.sqrt(total))
    diagonal = jax.random.uniform(diagonal_key, (N_GRP, N_DEV, OWNED), minval=0.5, maxval=1.5)
    row_number = (jnp.arange(N_GRP)[:, None, None] * N_DEV + jnp.arange(N_DEV)[None, :, None]) * OWNED + jnp.arange(OWNED)[None, None, :]
    identity = row_number[..., None] == jnp.arange(total)[None, None, None, :]
    return jnp.where(identity, off_part + diagonal[..., None], off_part)


def draw_face_rows(key, part):
    across_key, downward_key, priority_key = jax.random.split(jax.random.fold_in(key, 53), 3)
    lowest = max(FACE_ROWS // 4, 1)
    across = jax.random.randint(across_key, (N_GRP, N_DEV), lowest, FACE_ROWS + 1)
    downward = jax.random.randint(downward_key, (N_GRP, N_DEV), lowest, FACE_ROWS + 1)
    across = across.at[1, 0].set(FACE_ROWS).at[1, 1].set(FACE_ROWS)
    downward = downward.at[0, 1].set(FACE_ROWS).at[1, 1].set(FACE_ROWS)
    grp_pos = jnp.arange(N_GRP)[:, None]
    dev_pos = jnp.arange(N_DEV)[None, :]
    minus_dev = jnp.where(dev_pos > 0, jnp.roll(across, 1, axis=1), 0)
    plus_dev = jnp.where(dev_pos < N_DEV - 1, across, 0)
    minus_grp = jnp.where(grp_pos > 0, jnp.roll(downward, 1, axis=0), 0)
    plus_grp = jnp.where(grp_pos < N_GRP - 1, downward, 0)
    counts = jnp.stack([minus_dev, plus_dev, minus_grp, plus_grp], axis=2)
    live_slot = jnp.arange(FACE_ROWS)[None, None, None, :] < counts[..., None]
    live_slot = live_slot.reshape(N_GRP, N_DEV, 4 * FACE_ROWS)
    split_keys = jax.random.split(priority_key, N_GRP * N_DEV)
    priority = jax.vmap(lambda single: jax.random.permutation(single, 4 * FACE_ROWS))(split_keys)
    priority = priority.reshape(N_GRP, N_DEV, 4 * FACE_ROWS).astype(jnp.int32)
    ranking_key = jnp.where(live_slot, priority, 4 * FACE_ROWS + priority)
    ordering = jnp.argsort(ranking_key, axis=-1, stable=True)
    row_rank = jnp.argsort(ordering, axis=-1, stable=True).astype(jnp.int32)
    slot_rows = jnp.where(live_slot, row_rank, -1).astype(jnp.int32)
    return slot_rows.reshape(N_GRP, N_DEV, 4, FACE_ROWS)


def touch_ends(drawn, rng, low, high):
    extent = drawn.shape
    spot = [jax.random.randint(jax.random.fold_in(rng, axis), (), 0, extent[axis]) for axis in range(len(extent))]
    drawn = drawn.at[tuple(spot)].set(low)
    longest = extent.index(max(extent))
    spot[longest] = (spot[longest] + 1) % extent[longest]
    return drawn.at[tuple(spot)].set(high)


def shard_levels(stream_key, dims, cuts, least, top_value):
    factor_of = 1.0
    for dim, parts in cuts:
        heights = jax.random.uniform(jax.random.fold_in(jax.random.fold_in(stream_key, 6), dim), (parts,), jnp.float32, least / len(cuts), top_value / len(cuts))
        factor_of = factor_of * jnp.repeat(jnp.exp(heights), dims[dim] // parts).reshape((-1,) + (1,) * (len(dims) - 1 - dim))
    return factor_of


def gaussian(own_key, dims, scale, reach, cuts=(), kind=jnp.bfloat16):
    values = scale * jax.random.normal(own_key, dims, jnp.float32)
    if cuts:
        values = values * shard_levels(own_key, dims, cuts, -0.22, 0.18)
    return jnp.clip(values, -reach, reach).astype(kind)


def setup_inputs(seed: int = 0) -> dict:
    key_of = jax.random.split(jax.random.key(seed), 9)
    return {
        "objective": gaussian(key_of[0], (N_GRP, N_DEV, INTERFACE, COLUMNS), 4.0, 24.0, ((0, 8), (1, 32)), jnp.float32),
        "schur": draw_schur(jax.random.fold_in(key_of[8], 71), 0),
        "local_inverse": draw_local_inverse(jax.random.fold_in(key_of[8], 71), 0),
        "coarse_basis": gaussian(key_of[3], (N_GRP, N_DEV, COARSE_LOCAL, INTERFACE), (4 * INTERFACE) ** -0.5, 0.09375, ((0, 8), (1, 32)), jnp.float32),
        "coarse_inverse": draw_coarse_inverse(jax.random.fold_in(key_of[8], 71), 0),
        "stiffness": touch_ends(jax.random.randint(key_of[5], (N_GRP, N_DEV, INTERFACE), 1, 9), jax.random.fold_in(key_of[5], 1), 1, 8).astype(jnp.int32),
        "face_rows": draw_face_rows(jax.random.fold_in(key_of[8], 71), 0),
        "coarse_map": touch_ends(jax.random.randint(key_of[7], (N_GRP, N_DEV, COARSE_LOCAL), 0, N_GRP * OWNED), jax.random.fold_in(key_of[7], 1), 0, (N_GRP * OWNED) - 1).astype(jnp.int32),
    }


def slot_inverse(slot_rows):
    slot_count = 4 * FACE_ROWS
    slot_index = jnp.where(slot_rows < 0, INTERFACE, slot_rows).reshape(-1).astype(jnp.int32)
    empty = jnp.full((INTERFACE,), slot_count, jnp.int32)
    return empty.at[slot_index].set(jnp.arange(slot_count, dtype=jnp.int32), mode="drop")


def pack_one(values, slot_rows):
    slot_index = jnp.where(slot_rows < 0, INTERFACE, slot_rows).reshape(-1).astype(jnp.int32)
    return jnp.take(values, slot_index, axis=0, mode="fill", fill_value=0)


def unpack_one(received, inverse):
    return jnp.take(received, inverse, axis=0, mode="fill", fill_value=0)


def neighbour(values, face_rows, inverse):
    packed = jax.vmap(jax.vmap(pack_one))(values, face_rows)
    packed = packed.reshape(N_GRP, N_DEV, 4, FACE_ROWS, values.shape[-1])
    blank = jnp.zeros_like(packed[:, :, 0])
    from_left = jnp.concatenate([blank[:, :1], packed[:, :-1, 1]], axis=1)
    from_right = jnp.concatenate([packed[:, 1:, 0], blank[:, :1]], axis=1)
    from_above = jnp.concatenate([blank[:1], packed[:-1, :, 3]], axis=0)
    from_below = jnp.concatenate([packed[1:, :, 2], blank[:1]], axis=0)
    received = jnp.stack([from_left, from_right, from_above, from_below], axis=2)
    received = received.reshape(N_GRP, N_DEV, 4 * FACE_ROWS, values.shape[-1])
    return jax.vmap(jax.vmap(unpack_one))(received, inverse)


def reference(objective, schur, local_inverse, coarse_basis, coarse_inverse, stiffness, face_rows, coarse_map):
    highest = lax.Precision.HIGHEST
    inverse = jax.vmap(jax.vmap(slot_inverse))(face_rows)
    live_rows = (inverse < 4 * FACE_ROWS).astype(jnp.float32)[..., None]
    multiplicity = stiffness.astype(jnp.float32)[..., None]
    weight = live_rows * multiplicity / (multiplicity + neighbour(multiplicity, face_rows, inverse))
    onehot = (coarse_map[..., None] == jnp.arange(N_GRP * OWNED, dtype=jnp.int32)).astype(jnp.float32)
    inverse_matrix = coarse_inverse.reshape(COARSE, COARSE)
    adjoint = jnp.zeros(objective.shape, jnp.float32)
    for sweep_index in range(SWEEPS):
        if sweep_index == 0:
            remain = objective
        else:
            remain = objective - jnp.einsum("gdrc,gdrk->gdck", schur, adjoint, precision=highest)
        residual = live_rows * (remain + neighbour(remain, face_rows, inverse))
        weighted = weight * residual
        local_terms = jnp.einsum("gdlr,gdrk->gdlk", coarse_basis, weighted, precision=highest)
        spread_terms = jnp.einsum("gdlo,gdlk->gdok", onehot, local_terms, precision=highest)
        column_sums = jnp.sum(spread_terms, axis=0)
        coarse_residual = column_sums.reshape(N_DEV, N_GRP, OWNED, -1).transpose(1, 0, 2, 3).reshape(COARSE, -1)
        coarse_solution = jnp.dot(inverse_matrix.T, coarse_residual, precision=highest, preferred_element_type=jnp.float32)
        column_solution = coarse_solution.reshape(N_GRP, N_DEV, OWNED, -1).transpose(1, 0, 2, 3).reshape(N_DEV, N_GRP * OWNED, -1)
        local_solution = jnp.einsum("gdlo,dok->gdlk", onehot, column_solution, precision=highest)
        correction = jnp.einsum("gdlr,gdlk->gdrk", coarse_basis, local_solution, precision=highest)
        local_part = jnp.einsum("gdrc,gdrk->gdck", local_inverse, weighted, precision=highest)
        update = weight * (local_part + correction)
        adjoint = adjoint + update + neighbour(update, face_rows, inverse)
    return adjoint
```

```python
import jax
import jax.numpy as jnp
from jax import lax
from jax.sharding import PartitionSpec as P

INTERFACE = 1024
FACE_ROWS = 256
OWNED = 32
SWEEPS = 2
X_SIZE = 4


def split(value):
    high = lax.reduce_precision(value, 8, 7)
    return high.astype(jnp.bfloat16), (value - high).astype(jnp.bfloat16)


def dot(left, right, contract):
    return lax.dot_general(
        left,
        right,
        (contract, ((), ())),
        precision=lax.Precision.HIGH,
        preferred_element_type=jnp.float32,
    )


def select(onehot, value, contract):
    high, low = split(value)
    both = jnp.concatenate([high, low], axis=1)
    out = lax.dot_general(
        onehot, both, (contract, ((), ())), preferred_element_type=jnp.float32
    )
    width = value.shape[1]
    return out[:, :width] + out[:, width:]


ROWS = ((0,), (0,))
PLAIN = ((1,), (0,))


def on_device(
    objective, schur, local_inverse, coarse_basis, coarse_inverse, stiffness, face_rows, coarse_map
):
    n_grp, n_dev = lax.axis_size("grp"), lax.axis_size("dev")
    nx = X_SIZE
    nz = n_dev // nx
    grp = lax.axis_index("grp")
    dev = lax.axis_index("dev")
    x_pos, z_pos = dev % nx, dev // nx

    def shift_x(value, k):
        pairs = [(i, (i // nx) * nx + (i % nx + k) % nx) for i in range(n_dev)]
        return lax.ppermute(value, "dev", pairs)

    def shift_z(value, k):
        pairs = [(i, ((i // nx + k) % nz) * nx + i % nx) for i in range(n_dev)]
        return lax.ppermute(value, "dev", pairs)

    def group_gather(value):
        parts = [value]
        for k in range(1, n_grp):
            parts.append(lax.ppermute(value, "grp", [(i, i ^ k) for i in range(n_grp)]))
        return parts

    def exchange(faces):
        def pairs(size):
            return [(i, i + 1) for i in range(size - 1)]

        def back(size):
            return [(i + 1, i) for i in range(size - 1)]

        return [
            lax.ppermute(faces[1], "dev", pairs(n_dev)),
            lax.ppermute(faces[0], "dev", back(n_dev)),
            lax.ppermute(faces[3], "grp", pairs(n_grp)),
            lax.ppermute(faces[2], "grp", back(n_grp)),
        ]

    def neighbour(values):
        faces = values.reshape(4, FACE_ROWS, values.shape[-1])
        return jnp.concatenate(exchange([faces[p] for p in range(4)]), axis=0)

    slots = face_rows[0, 0].reshape(-1)
    row_ids = jnp.arange(INTERFACE, dtype=jnp.int32)
    pack = (slots[:, None] == row_ids[None, :]).astype(jnp.bfloat16)

    mult = stiffness[0, 0].astype(jnp.bfloat16)
    mult_slots = lax.dot_general(
        mult[None, :], pack, (((1,), (1,)), ((), ())), preferred_element_type=jnp.float32
    )
    gradient = select(pack, objective[0, 0], PLAIN)
    columns = gradient.shape[1]
    first = []
    for p in range(4):
        face = gradient[p * FACE_ROWS : (p + 1) * FACE_ROWS]
        extra = mult_slots[:, p * FACE_ROWS : (p + 1) * FACE_ROWS]
        extra = jnp.pad(extra, ((0, 7), (0, 0)))
        first.append(jnp.concatenate([face, extra], axis=0))
    arrived = exchange(first)

    basis = select(pack, coarse_basis[0, 0].T, PLAIN)
    local_map = coarse_map[0, 0]
    tile = coarse_inverse.reshape(-1, coarse_inverse.shape[3])
    tile_t = tile.T.reshape(nz, nx, OWNED, tile.shape[0])
    twice = jnp.concatenate([tile_t, tile_t], axis=1)
    tile_t = lax.dynamic_slice_in_dim(twice, x_pos, nx, 1)
    twice = jnp.concatenate([tile_t, tile_t], axis=0)
    tile_t = lax.dynamic_slice_in_dim(twice, z_pos, nz, 0)
    tile_t = tile_t.transpose(1, 0, 2, 3).reshape(nx, nz * OWNED, tile.shape[0])

    coarse_rows = n_grp * OWNED
    rel_map = ((local_map // OWNED) ^ grp) * OWNED + local_map % OWNED
    fetch = (rel_map[:, None] == jnp.arange(coarse_rows, dtype=jnp.int32)[None, :]).astype(
        jnp.bfloat16
    )

    mult_here = mult_slots.reshape(-1)[:, None]
    mult_there = jnp.concatenate([a[FACE_ROWS, :] for a in arrived])[:, None]
    total = mult_here + mult_there
    weight = jnp.where(total > 0, mult_here / jnp.maximum(total, 1), 0)
    received = jnp.concatenate([a[:FACE_ROWS] for a in arrived], axis=0)

    adjoint = None
    spread = None
    for sweep in range(SWEEPS):
        if sweep == 0:
            residual = gradient + received
        else:
            rows = select(pack, adjoint, ROWS)
            remain = gradient - select(pack, dot(schur[0, 0], rows, ROWS), PLAIN)
            residual = remain + neighbour(remain)
        weighted = weight * residual
        terms = dot(basis, weighted, ROWS)
        if sweep == 0:
            extra = jnp.zeros((8, columns), jnp.float32)
            extra = extra.at[0, : local_map.shape[0]].set(local_map.astype(jnp.float32))
            parts = group_gather(jnp.concatenate([terms, extra], axis=0))
            maps = jnp.concatenate([p[terms.shape[0], : terms.shape[0]] for p in parts])
            spread = (
                jnp.arange(coarse_rows, dtype=jnp.float32)[:, None] == maps[None, :]
            ).astype(jnp.bfloat16)
            parts = [p[: terms.shape[0]] for p in parts]
        else:
            parts = group_gather(terms)
        column_residual = select(spread, jnp.concatenate(parts, axis=0), PLAIN)

        blocks = [None] * nx
        sent = []
        for k in (2, 1, 3, 0):
            blocks[k] = dot(tile_t[k], column_residual, PLAIN)
            if k:
                sent.append(shift_x(blocks[k], k))
        local_rows = dot(local_inverse[0, 0], select(pack, weighted, ROWS), ROWS)
        local_part = select(pack, local_rows, PLAIN)
        acc = blocks[0] + sent[0] + sent[1] + sent[2]
        acc = acc.reshape(nz, OWNED, columns)
        owned = acc[0]
        for k in (4, 3, 5, 2, 6, 1, 7):
            owned = owned + shift_z(acc[k], k)
        solution_parts = jnp.concatenate(group_gather(owned), axis=0)
        local_solution = select(fetch, solution_parts, PLAIN)
        correction = dot(basis, local_solution, PLAIN)
        update = weight * (local_part + correction)
        update = update + neighbour(update)
        adjoint = update if adjoint is None else adjoint + update
    return select(pack, adjoint, ROWS)[None, None]


def solution(mesh):
    return jax.shard_map(
        on_device,
        mesh=mesh,
        in_specs=(
            P("grp", "dev", None, None),
            P("grp", "dev", None, None),
            P("grp", "dev", None, None),
            P("grp", "dev", None, None),
            P(None, "dev", None, "grp"),
            P("grp", "dev", None),
            P("grp", "dev", None, None),
            P("grp", "dev", None),
        ),
        out_specs=P("grp", "dev", None, None),
        check_vma=False,
    )
```

```python
import functools

import jax
import jax.numpy as jnp
from jax import lax
from jax.experimental import pallas as pl
from jax.experimental.pallas import tpu as pltpu
from jax.sharding import PartitionSpec as P

INTERFACE = 1024
FACE_ROWS = 256
COLUMNS = 256
OWNED = 32
LOCAL = 64
SWEEPS = 2
X_SIZE = 4
TILE = 256
FACES = 4
TERM_ROWS = LOCAL + 8
MULT_ROWS = COLUMNS + 8
LIFT_ROWS = COLUMNS + LOCAL

NN = (((1,), (0,)), ((), ()))
NT = (((1,), (1,)), ((), ()))
TN = (((0,), (0,)), ((), ()))

VMEM = pl.BlockSpec(memory_space=pltpu.VMEM)
SMEM = pl.BlockSpec(memory_space=pltpu.SMEM)


def shaped(*shape, dtype=jnp.float32):
    return jax.ShapeDtypeStruct(shape, dtype)


def params():
    return pltpu.CompilerParams(vmem_limit_bytes=40 << 20)


def cost(flops, moved):
    return pl.CostEstimate(flops=flops, bytes_accessed=moved, transcendentals=0)


def split(value):
    high = value.astype(jnp.bfloat16)
    low = (value - high.astype(jnp.float32)).astype(jnp.bfloat16)
    return high, low


def mul(left, right, dims):
    return lax.dot_general(left, right, dims, preferred_element_type=jnp.float32)


def mul3(left, right, dims):
    left_high, left_low = left
    right_high, right_low = right
    return (
        mul(left_high, right_low, dims)
        + mul(left_low, right_high, dims)
        + mul(left_high, right_high, dims)
    )


def row_tile(slots_ref, t):
    rows = lax.broadcasted_iota(jnp.int32, (TILE, INTERFACE), 0) + t * TILE
    return (rows == slots_ref[...]).astype(jnp.float32).astype(jnp.bfloat16)


def tile_at(t):
    return pl.ds(pl.multiple_of(t * TILE, TILE), TILE)


def face_at(p):
    return slice(p * FACE_ROWS, (p + 1) * FACE_ROWS)


def pack_kernel(slots_ref, objective_ref, small_ref, basis_ref, *rest):
    outs, (acc, acc_small) = rest[:FACES], rest[FACES:]
    acc[...] = jnp.zeros_like(acc)
    acc_small[...] = jnp.zeros_like(acc_small)

    @pl.loop(0, INTERFACE // TILE)
    def _(t):
        onehot = row_tile(slots_ref, t)
        high, low = split(objective_ref[tile_at(t), :].T)
        acc[...] += mul(high, onehot, NN) + mul(low, onehot, NN)
        high, low = split(small_ref[:, tile_at(t)])
        acc_small[...] += mul(high, onehot, NN) + mul(low, onehot, NN)

    basis_ref[...] = acc_small[:LOCAL]
    for p in range(FACES):
        outs[p][:COLUMNS] = acc[:, face_at(p)]
        outs[p][COLUMNS:] = acc_small[LOCAL:, face_at(p)]


def pack_call(slots, objective, small):
    return pl.pallas_call(
        pack_kernel,
        out_shape=[shaped(LOCAL, INTERFACE)] + [shaped(MULT_ROWS, FACE_ROWS)] * FACES,
        in_specs=[VMEM] * 3,
        out_specs=[VMEM] * 5,
        scratch_shapes=[
            pltpu.VMEM((COLUMNS, INTERFACE), jnp.float32),
            pltpu.VMEM((TERM_ROWS, INTERFACE), jnp.float32),
        ],
        compiler_params=params(),
        cost_estimate=cost(3 << 30, 4 << 20),
        name="pack",
    )(slots, objective, small)


def weigh_kernel(first, *refs):
    here, there = refs[:FACES], refs[FACES : 2 * FACES]
    basis_ref, map_ref = refs[2 * FACES : 2 * FACES + 2]
    weighted_ref, terms_ref = refs[2 * FACES + 2 : 2 * FACES + 4]
    terms = jnp.zeros((LOCAL, COLUMNS), jnp.float32)
    for p in range(FACES):
        mine = here[p][COLUMNS : COLUMNS + 1]
        total = mine + there[p][COLUMNS : COLUMNS + 1]
        weight = jnp.where(total > 0, mine / jnp.maximum(total, 1.0), 0.0)
        weighted = weight * (here[p][:COLUMNS] + there[p][:COLUMNS])
        weighted_ref[:, face_at(p)] = weighted
        basis = basis_ref[:, face_at(p)]
        terms = terms + mul3(split(basis), split(weighted), NT)
        if first:
            weight_ref, lift_ref = refs[2 * FACES + 4 :]
            weight_ref[:, face_at(p)] = jnp.broadcast_to(weight, (8, FACE_ROWS))
            lift_ref[:, face_at(p)] = basis * weight
    terms_ref[:LOCAL] = terms
    terms_ref[LOCAL:] = map_ref[...]


def weigh_call(here, there, basis, map_row, first):
    out = [shaped(COLUMNS, INTERFACE), shaped(TERM_ROWS, COLUMNS)]
    if first:
        out += [shaped(8, INTERFACE), shaped(LOCAL, INTERFACE)]
    return pl.pallas_call(
        functools.partial(weigh_kernel, first),
        out_shape=out,
        in_specs=[VMEM] * (2 * FACES + 2),
        out_specs=[VMEM] * len(out),
        compiler_params=params(),
        cost_estimate=cost(100 << 20, 3 << 20),
        name="weigh",
    )(*here, *there, basis, map_row)


def coarse_kernel(n_grp, nz, nx, x_ref, half_ref, other_ref, high_ref, low_ref, *rest):
    outs, scratch = rest[:nx], rest[nx]
    dofs = n_grp * OWNED
    column = jnp.zeros((dofs, COLUMNS), jnp.float32)
    rows = lax.broadcasted_iota(jnp.int32, (dofs, LOCAL), 0).astype(jnp.float32)
    for ref in (half_ref, other_ref):
        for j in range(n_grp // 2):
            at = j * TERM_ROWS
            names = ref[at + LOCAL : at + LOCAL + 1, :LOCAL]
            onehot = (rows == names).astype(jnp.float32).astype(jnp.bfloat16)
            high, low = split(ref[at : at + LOCAL, :])
            column = column + mul(onehot, high, NN) + mul(onehot, low, NN)
    right = split(column)
    chunk = nx * OWNED
    x_pos = x_ref[0]

    @pl.loop(0, nz)
    def _(z):
        at = pl.ds(pl.multiple_of(z * chunk, chunk), chunk)
        scratch[...] = mul3((high_ref[at, :], low_ref[at, :]), right, NN)
        for k in range(nx):
            start = pl.multiple_of((x_pos ^ k) * OWNED, OWNED)
            outs[k][pl.ds(pl.multiple_of(z * OWNED, OWNED), OWNED), :] = scratch[
                pl.ds(start, OWNED), :
            ]


def coarse_call(x_pos, half, other, high, low, n_grp, nz, nx):
    return pl.pallas_call(
        functools.partial(coarse_kernel, n_grp, nz, nx),
        out_shape=[shaped(nz * OWNED, COLUMNS)] * nx,
        in_specs=[SMEM] + [VMEM] * 4,
        out_specs=[VMEM] * nx,
        scratch_shapes=[pltpu.VMEM((nx * OWNED, COLUMNS), jnp.float32)],
        compiler_params=params(),
        cost_estimate=cost(600 << 20, 3 << 20),
        name="coarse",
    )(x_pos, half, other, high, low)


def fetch_kernel(wanted_ref, half_ref, other_ref, *outs):
    count = half_ref.shape[0]
    ids = lax.broadcasted_iota(jnp.int32, (LOCAL, count), 1)
    left, right = split(half_ref[...]), split(other_ref[...])
    for i, out in enumerate(outs):
        wanted = wanted_ref[i * LOCAL : (i + 1) * LOCAL, :]
        near = (wanted == ids).astype(jnp.float32).astype(jnp.bfloat16)
        far = (wanted == ids + count).astype(jnp.float32).astype(jnp.bfloat16)
        out[...] = (
            mul(near, left[0], NN)
            + mul(far, right[0], NN)
            + mul(near, left[1], NN)
            + mul(far, right[1], NN)
        )


def fetch_call(wanted, half, other):
    return pl.pallas_call(
        fetch_kernel,
        out_shape=[shaped(LOCAL, COLUMNS)] * 3,
        in_specs=[VMEM] * 3,
        out_specs=[VMEM] * 3,
        compiler_params=params(),
        cost_estimate=cost(100 << 20, 1 << 20),
        name="fetch",
    )(wanted, half, other)


def unpack(slots_ref, value, high_ref, low_ref):
    high, low = split(value)

    @pl.loop(0, INTERFACE // TILE)
    def _(t):
        onehot = row_tile(slots_ref, t)
        rows = mul(high, onehot, NT) + mul(low, onehot, NT)
        high_ref[:, tile_at(t)], low_ref[:, tile_at(t)] = split(rows)


def apply_tile(slots_ref, matrix_ref, high_ref, low_ref, acc):
    step = pl.program_id(0)

    @pl.when(step == 0)
    def _():
        acc[...] = jnp.zeros_like(acc)

    rows = mul3((high_ref[...], low_ref[...]), split(matrix_ref[...]), NN)
    high, low = split(rows)
    onehot = row_tile(slots_ref, step)
    acc[...] += mul(high, onehot, NN) + mul(low, onehot, NN)


def whole(shape):
    return pl.BlockSpec(shape, lambda i: (0,) * len(shape))


def columns_of(shape):
    return pl.BlockSpec((shape[0], TILE), lambda i: (0, i))


APPLY_SCRATCH = [
    pltpu.VMEM((COLUMNS, INTERFACE), jnp.bfloat16),
    pltpu.VMEM((COLUMNS, INTERFACE), jnp.bfloat16),
    pltpu.VMEM((COLUMNS, INTERFACE), jnp.float32),
]


def local_kernel(first, slots_ref, weighted_ref, matrix_ref, weight_ref, lift_ref, *rest):
    outs, (high, low, acc) = rest[:FACES], rest[FACES:]
    step = pl.program_id(0)

    @pl.when(step == 0)
    def _():
        unpack(slots_ref, weighted_ref[...], high, low)

    apply_tile(slots_ref, matrix_ref, high, low, acc)

    @pl.when(step == pl.num_programs(0) - 1)
    def _():
        for p in range(FACES):
            outs[p][:COLUMNS] = weight_ref[:1, face_at(p)] * acc[:, face_at(p)]
            if first:
                outs[p][COLUMNS:] = lift_ref[:, face_at(p)]


def local_call(slots, weighted, matrix, weight, lift, first):
    out = [shaped(LIFT_ROWS if first else COLUMNS, FACE_ROWS)] * FACES
    return pl.pallas_call(
        functools.partial(local_kernel, first),
        grid=(INTERFACE // TILE,),
        out_shape=out,
        in_specs=[
            whole(slots.shape),
            whole(weighted.shape),
            columns_of(matrix.shape),
            whole(weight.shape),
            whole(lift.shape),
        ],
        out_specs=[whole(o.shape) for o in out],
        scratch_shapes=APPLY_SCRATCH,
        compiler_params=params(),
        cost_estimate=cost(4 << 30, 8 << 20),
        name="local",
    )(slots, weighted, matrix, weight, lift)


def adjoint_face(p, near, far, lift_near, lift_far, own, around):
    change = mul3(own, split(lift_near[p][...]), TN)
    change = change + mul3(split(around[p][...]), split(lift_far[p][...]), TN)
    return near[p][...] + far[p][...] + change


def middle_kernel(slots_ref, *refs):
    groups = [refs[i * FACES : (i + 1) * FACES] for i in range(6)]
    near, far, lift_near, lift_far, around, gradient = groups
    own_ref, matrix_ref, adjoint_ref = refs[6 * FACES : 6 * FACES + 3]
    outs, (high, low, acc) = refs[6 * FACES + 3 : 7 * FACES + 3], refs[7 * FACES + 3 :]
    step = pl.program_id(0)

    @pl.when(step == 0)
    def _():
        own = split(own_ref[...])
        for p in range(FACES):
            adjoint_ref[:, face_at(p)] = adjoint_face(
                p, near, far, lift_near, lift_far, own, around
            )
        unpack(slots_ref, adjoint_ref[...], high, low)

    apply_tile(slots_ref, matrix_ref, high, low, acc)

    @pl.when(step == pl.num_programs(0) - 1)
    def _():
        for p in range(FACES):
            outs[p][:COLUMNS] = gradient[p][:COLUMNS] - acc[:, face_at(p)]
            outs[p][COLUMNS:] = gradient[p][COLUMNS:]


def top(i):
    return (0, 0)


def tail(i):
    return (COLUMNS // LOCAL, 0)


def update_specs():
    body = pl.BlockSpec((COLUMNS, FACE_ROWS), top)
    lift = pl.BlockSpec((LOCAL, FACE_ROWS), tail)
    around = pl.BlockSpec((LOCAL, COLUMNS), top)
    return [body] * (2 * FACES) + [lift] * (2 * FACES) + [around] * FACES


def middle_call(slots, near, far, lift_near, lift_far, around, gradient, own, matrix):
    out = [shaped(COLUMNS, INTERFACE)] + [shaped(MULT_ROWS, FACE_ROWS)] * FACES
    return pl.pallas_call(
        middle_kernel,
        grid=(INTERFACE // TILE,),
        out_shape=out,
        in_specs=[whole(slots.shape)]
        + update_specs()
        + [whole(gradient[0].shape)] * FACES
        + [whole(own.shape), columns_of(matrix.shape)],
        out_specs=[whole(o.shape) for o in out],
        scratch_shapes=APPLY_SCRATCH,
        compiler_params=params(),
        cost_estimate=cost(4 << 30, 12 << 20),
        name="middle",
    )(slots, *near, *far, *lift_near, *lift_far, *around, *gradient, own, matrix)


def last_kernel(slots_ref, *refs):
    groups = [refs[i * FACES : (i + 1) * FACES] for i in range(5)]
    near, far, lift_near, lift_far, around = groups
    own_ref, adjoint_ref, out_ref, high, low = refs[5 * FACES :]
    step = pl.program_id(0)

    @pl.when(step == 0)
    def _():
        own = split(own_ref[...])
        for p in range(FACES):
            value = adjoint_ref[:, face_at(p)] + adjoint_face(
                p, near, far, lift_near, lift_far, own, around
            )
            high[:, face_at(p)], low[:, face_at(p)] = split(value)

    onehot = row_tile(slots_ref, step)
    out_ref[...] = mul(onehot, high[...], NT) + mul(onehot, low[...], NT)


def last_call(slots, near, far, lift_near, lift_far, around, own, adjoint):
    return pl.pallas_call(
        last_kernel,
        grid=(INTERFACE // TILE,),
        out_shape=shaped(INTERFACE, COLUMNS),
        in_specs=[whole(slots.shape)]
        + update_specs()
        + [whole(own.shape), whole(adjoint.shape)],
        out_specs=pl.BlockSpec((TILE, COLUMNS), lambda i: (i, 0)),
        scratch_shapes=APPLY_SCRATCH[:2],
        compiler_params=params(),
        cost_estimate=cost(1 << 30, 6 << 20),
        name="last",
    )(slots, *near, *far, *lift_near, *lift_far, *around, own, adjoint)


def on_device(
    objective, schur, local_inverse, coarse_basis, coarse_inverse, stiffness, face_rows, coarse_map
):
    n_grp, n_dev = lax.axis_size("grp"), lax.axis_size("dev")
    nx = X_SIZE
    nz = n_dev // nx
    grp = lax.axis_index("grp")
    x_pos = (lax.axis_index("dev") % nx).astype(jnp.int32).reshape(1)
    z_groups = [[z * nx + x for z in range(nz)] for x in range(nx)]
    half_size = n_grp // 2

    def place(other):
        j = other ^ grp
        return j // 2 + half_size * (j % 2)

    def swap(value, axis, k):
        size = lax.axis_size(axis)
        return lax.ppermute(value, axis, [(i, i ^ k) for i in range(size)])

    def group_gather(value):
        parts = [value] + [swap(value, "grp", k) for k in range(2, n_grp, 2)]
        half = jnp.concatenate(parts, axis=0)
        return half, swap(half, "grp", 1)

    def pairs(axis):
        return [(i, i + 1) for i in range(lax.axis_size(axis) - 1)]

    def back(axis):
        return [(i + 1, i) for i in range(lax.axis_size(axis) - 1)]

    def exchange(faces):
        return [
            lax.ppermute(faces[1], "dev", pairs("dev")),
            lax.ppermute(faces[0], "dev", back("dev")),
            lax.ppermute(faces[3], "grp", pairs("grp")),
            lax.ppermute(faces[2], "grp", back("grp")),
        ]

    slots = face_rows[0, 0].reshape(1, -1)
    local_map = coarse_map[0, 0]
    multiplicity = jnp.pad(stiffness[0].astype(jnp.float32), ((0, 7), (0, 0)))
    small = jnp.concatenate([coarse_basis[0, 0], multiplicity], axis=0)
    basis, *gradient = pack_call(slots, objective[0, 0], small)
    arrived = exchange(gradient)

    map_row = jnp.zeros((8, COLUMNS), jnp.float32)
    map_row = map_row.at[0, :LOCAL].set(local_map.astype(jnp.float32))
    tile = coarse_inverse.reshape(-1, coarse_inverse.shape[3]).T
    tile_high = lax.reduce_precision(tile, 8, 7)
    tile_low = (tile - tile_high).astype(jnp.bfloat16)
    tile_high = tile_high.astype(jnp.bfloat16)

    weighted, terms, weight, lift = weigh_call(gradient, arrived, basis, map_row, True)
    wanted = None
    adjoint = None
    lift_near = lift_far = None
    for sweep in range(SWEEPS):
        first = sweep == 0
        half, other = group_gather(terms)
        if first:
            maps = jnp.concatenate([half, other], axis=0).reshape(n_grp, TERM_ROWS, COLUMNS)
            maps = maps[:, LOCAL, :LOCAL]
            above = lax.dynamic_slice_in_dim(maps, place(jnp.maximum(grp - 1, 0)), 1, 0)[0]
            below = lax.dynamic_slice_in_dim(maps, place(jnp.minimum(grp + 1, n_grp - 1)), 1, 0)[0]
            wanted = jnp.concatenate([local_map, above.astype(jnp.int32), below.astype(jnp.int32)])
            wanted = (place(wanted // OWNED) * OWNED + wanted % OWNED)[:, None]
        blocks = coarse_call(x_pos, half, other, tile_high, tile_low, n_grp, nz, nx)
        sent = [swap(blocks[k], "dev", k) for k in (2, 1, 3)]
        near = local_call(slots, weighted, local_inverse[0, 0], weight, lift, first)
        total = blocks[0] + sent[0] + sent[1] + sent[2]
        total = lax.all_to_all(
            total.reshape(nz, OWNED, COLUMNS), "dev", 0, 0, axis_index_groups=z_groups, tiled=True
        )
        owned = total.sum(0)
        far = exchange(near)
        if first:
            lift_near, lift_far = near, far
        own, above, below = fetch_call(wanted, *group_gather(owned))
        around = [
            lax.ppermute(own, "dev", pairs("dev")),
            lax.ppermute(own, "dev", back("dev")),
            above,
            below,
        ]
        if first:
            adjoint, *remain = middle_call(
                slots, near, far, lift_near, lift_far, around, gradient, own, schur[0, 0]
            )
            weighted, terms = weigh_call(remain, exchange(remain), basis, map_row, False)
        else:
            out = last_call(slots, near, far, lift_near, lift_far, around, own, adjoint)
    return out[None, None]


def solution(mesh):
    return jax.shard_map(
        on_device,
        mesh=mesh,
        in_specs=(
            P("grp", "dev", None, None),
            P("grp", "dev", None, None),
            P("grp", "dev", None, None),
            P("grp", "dev", None, None),
            P(None, "dev", None, "grp"),
            P("grp", "dev", None),
            P("grp", "dev", None, None),
            P("grp", "dev", None),
        ),
        out_specs=P("grp", "dev", None, None),
        check_vma=False,
    )
```

```python
import functools

import jax
import jax.numpy as jnp
from jax import lax
from jax.experimental import pallas as pl
from jax.experimental.pallas import tpu as pltpu
from jax.sharding import PartitionSpec as P

INTERFACE = 1024
FACE_ROWS = 256
COLUMNS = 256
OWNED = 32
LOCAL = 64
SWEEPS = 2
X_SIZE = 4
TILE = 256
FACES = 4
TERM_ROWS = LOCAL + 8
MULT_ROWS = COLUMNS + 8
LIFT_ROWS = COLUMNS + LOCAL

NN = (((1,), (0,)), ((), ()))
NT = (((1,), (1,)), ((), ()))
TN = (((0,), (0,)), ((), ()))

VMEM = pl.BlockSpec(memory_space=pltpu.VMEM)
SMEM = pl.BlockSpec(memory_space=pltpu.SMEM)
ANY = pl.BlockSpec(memory_space=pl.ANY)
HBM = "hbm"


def shaped(*shape, dtype=jnp.float32):
    return jax.ShapeDtypeStruct(shape, dtype)


def in_hbm(*shape, dtype=jnp.float32):
    return pltpu.HBM(shape, dtype)


def params():
    return pltpu.CompilerParams(vmem_limit_bytes=20 << 20)


def cost(flops, moved):
    return pl.CostEstimate(flops=flops, bytes_accessed=moved, transcendentals=0)


def call(kernel, name, out_shape, flops, moved, in_specs, scratch=()):
    outs = [VMEM if isinstance(o, jax.ShapeDtypeStruct) else ANY for o in out_shape]
    function = pl.pallas_call(
        kernel,
        out_shape=out_shape,
        in_specs=[ANY if spec is HBM else spec for spec in in_specs],
        out_specs=outs,
        scratch_shapes=scratch,
        compiler_params=params(),
        cost_estimate=cost(flops, moved),
        name=name,
    )

    def run(*values):
        values = [
            pltpu.with_memory_space_constraint(value, pltpu.HBM) if spec is HBM else value
            for value, spec in zip(values, in_specs)
        ]
        return function(*values)

    return run


def split(value):
    high = value.astype(jnp.bfloat16)
    low = (value - high.astype(jnp.float32)).astype(jnp.bfloat16)
    return high, low


def mul(left, right, dims):
    return lax.dot_general(left, right, dims, preferred_element_type=jnp.float32)


def mul3(left, right, dims):
    left_high, left_low = left
    right_high, right_low = right
    return (
        mul(left_high, right_low, dims)
        + mul(left_low, right_high, dims)
        + mul(left_high, right_high, dims)
    )


def folded(value):
    return value[:COLUMNS] + value[COLUMNS:]


def tile_at(t):
    return pl.ds(pl.multiple_of(t * TILE, TILE), TILE)


def face_at(p):
    return slice(p * FACE_ROWS, (p + 1) * FACE_ROWS)


def put(ref, at, value):
    ref[:COLUMNS, at], ref[COLUMNS:, at] = split(value)


PAIR = pltpu.VMEM((2 * COLUMNS, INTERFACE), jnp.bfloat16)
STEPS = INTERFACE // TILE
BASIS_AT = 2 * COLUMNS
MULT_AT = BASIS_AT + 2 * LOCAL


def fetched(source, target, sem):
    copy = pltpu.make_async_copy(source, target, sem)
    copy.start()
    return copy


def pack_kernel(
    odd_ref, slots_in, objective_in, basis_in, mult_in, basis_ref, onehot_ref, *rest
):
    outs = rest[:FACES]
    slots, staged, basis, mult, sems, left = rest[FACES:]
    slots_copy = fetched(slots_in, slots, sems.at[STEPS])
    small = [
        fetched(basis_in, basis, sems.at[STEPS + 1]),
        fetched(mult_in, mult, sems.at[STEPS + 2]),
    ]
    copies = [
        fetched(objective_in.at[t * TILE : (t + 1) * TILE], staged.at[t], sems.at[t])
        for t in range(STEPS)
    ]
    slots_copy.wait()
    odd_dev, odd_grp = odd_ref[0] == 1, odd_ref[1] == 1
    lines = [slots[p : p + 1] for p in range(FACES)]
    lines = [
        jnp.where(odd_dev, lines[0], lines[1]),
        jnp.where(odd_dev, lines[1], lines[0]),
        jnp.where(odd_grp, lines[2], lines[3]),
        jnp.where(odd_grp, lines[3], lines[2]),
    ]
    for p in range(FACES):
        rows = lax.broadcasted_iota(jnp.int32, (INTERFACE, FACE_ROWS), 0)
        onehot_ref[:, face_at(p)] = (
            (rows == lines[p]).astype(jnp.float32).astype(jnp.bfloat16)
        )
    for copy in small:
        copy.wait()
    left[BASIS_AT : BASIS_AT + LOCAL], left[BASIS_AT + LOCAL : MULT_AT] = split(basis[...])
    left[MULT_AT:] = jnp.broadcast_to(mult[...].astype(jnp.float32), (16, INTERFACE)).astype(
        jnp.bfloat16
    )
    for t in range(STEPS):
        copies[t].wait()
        at = slice(t * TILE, (t + 1) * TILE)
        left[:COLUMNS, at], left[COLUMNS:BASIS_AT, at] = split(staged[t].T)
    for p in range(FACES):
        out = mul(left[...], onehot_ref[:, face_at(p)], NN)
        outs[p][:COLUMNS] = folded(out[:BASIS_AT])
        outs[p][COLUMNS:] = out[MULT_AT : MULT_AT + 8]
        basis_ref[:, face_at(p)] = out[BASIS_AT : BASIS_AT + LOCAL] + out[BASIS_AT + LOCAL : MULT_AT]


def pack_call(odd, slots, objective, basis, mult):
    return call(
        pack_kernel,
        "pack",
        [shaped(LOCAL, INTERFACE), shaped(INTERFACE, INTERFACE, dtype=jnp.bfloat16)]
        + [shaped(MULT_ROWS, FACE_ROWS)] * FACES,
        2 << 30,
        4 << 20,
        [SMEM] + [HBM] * 4,
        scratch=[
            pltpu.VMEM((FACES, FACE_ROWS), jnp.int32),
            pltpu.VMEM((STEPS, TILE, COLUMNS), jnp.float32),
            pltpu.VMEM((LOCAL, INTERFACE), jnp.float32),
            pltpu.VMEM((1, INTERFACE), jnp.int32),
            pltpu.SemaphoreType.DMA((STEPS + 3,)),
            pltpu.VMEM((MULT_AT + 16, INTERFACE), jnp.bfloat16),
        ],
    )(odd, slots, objective, basis, mult)


def tile_kernel(tile_in, high_out, low_out, staged, sems, high, low, out_sems):
    copies = [
        fetched(tile_in.at[:, t * TILE : (t + 1) * TILE], staged.at[t], sems.at[t])
        for t in range(STEPS)
    ]
    outs = []
    for t in range(STEPS):
        copies[t].wait()
        at = slice(t * TILE, (t + 1) * TILE)
        high[at], low[at] = split(staged[t].T)
        outs.append(fetched(high.at[at], high_out.at[at], out_sems.at[0, t]))
        outs.append(fetched(low.at[at], low_out.at[at], out_sems.at[1, t]))
    for copy in outs:
        copy.wait()


def tile_call(tile):
    rows, width = tile.shape
    half = pltpu.VMEM((width, rows), jnp.bfloat16)
    return call(
        tile_kernel,
        "tile",
        [in_hbm(width, rows, dtype=jnp.bfloat16)] * 2,
        1 << 20,
        4 << 20,
        [HBM],
        scratch=[
            pltpu.VMEM((STEPS, rows, TILE), jnp.float32),
            pltpu.SemaphoreType.DMA((STEPS,)),
            half,
            half,
            pltpu.SemaphoreType.DMA((2, STEPS)),
        ],
    )(tile)


def join_kernel(*refs):
    rows = refs[0].shape[0]
    for i, ref in enumerate(refs[:-1]):
        refs[-1][i * rows : (i + 1) * rows] = ref[...]


def join_call(parts):
    rows, width = parts[0].shape
    (out,) = call(
        join_kernel,
        "join",
        [shaped(len(parts) * rows, width)],
        1 << 20,
        1 << 19,
        [VMEM] * len(parts),
    )(*parts)
    return out


def weigh_kernel(first, *refs):
    here, there = refs[:FACES], refs[FACES : 2 * FACES]
    basis_ref, map_ref = refs[2 * FACES : 2 * FACES + 2]
    weighted_out, terms_ref = refs[2 * FACES + 2 : 2 * FACES + 4]
    if first:
        weight_ref, lift_out, weighted_ref, sems, lift_ref = refs[2 * FACES + 4 :]
    else:
        weighted_ref, sems = refs[2 * FACES + 4 :]
    terms = jnp.zeros((LOCAL, COLUMNS), jnp.float32)
    copies = []
    for p in range(FACES):
        mine = here[p][COLUMNS : COLUMNS + 1]
        total = mine + there[p][COLUMNS : COLUMNS + 1]
        weight = jnp.where(total > 0, mine / jnp.maximum(total, 1.0), 0.0)
        weighted = weight * (here[p][:COLUMNS] + there[p][:COLUMNS])
        high, low = split(weighted)
        weighted_ref[:COLUMNS, face_at(p)] = high
        weighted_ref[COLUMNS:, face_at(p)] = low
        at = (slice(None), face_at(p))
        copies.append(fetched(weighted_ref.at[at], weighted_out.at[at], sems.at[p]))
        basis = basis_ref[:, face_at(p)]
        terms = terms + mul3(split(basis), (high, low), NT)
        if first:
            weight_ref[:, face_at(p)] = jnp.broadcast_to(weight, (8, FACE_ROWS))
            lift_ref[:, face_at(p)] = basis * weight
            copies.append(fetched(lift_ref.at[at], lift_out.at[at], sems.at[FACES + p]))
    terms_ref[:LOCAL] = terms
    terms_ref[LOCAL:] = map_ref[...]
    for copy in copies:
        copy.wait()


def weigh_call(here, there, basis, map_row, first):
    out = [in_hbm(2 * COLUMNS, INTERFACE, dtype=jnp.bfloat16), shaped(TERM_ROWS, COLUMNS)]
    scratch = [PAIR, pltpu.SemaphoreType.DMA((2 * FACES,))]
    if first:
        out += [shaped(8, INTERFACE), in_hbm(LOCAL, INTERFACE)]
        scratch += [pltpu.VMEM((LOCAL, INTERFACE), jnp.float32)]
    return call(
        functools.partial(weigh_kernel, first),
        "weigh",
        out,
        100 << 20,
        2 << 20,
        [VMEM] * (2 * FACES + 2),
        scratch=scratch,
    )(*here, *there, basis, map_row)


def coarse_kernel(n_grp, nz, nx, x_ref, half_ref, other_ref, high_in, low_in, *rest):
    outs, (scratch, right, high_ref, low_ref, sems) = rest[:nx], rest[nx:]
    high_copy = fetched(high_in, high_ref, sems.at[0])
    low_copy = fetched(low_in, low_ref, sems.at[1])
    dofs = n_grp * OWNED
    column = jnp.zeros((dofs, 2 * COLUMNS), jnp.float32)
    rows = lax.broadcasted_iota(jnp.int32, (dofs, LOCAL), 0).astype(jnp.float32)
    for ref in (half_ref, other_ref):
        for j in range(n_grp // 2):
            at = j * TERM_ROWS
            names = ref[at + LOCAL : at + LOCAL + 1, :LOCAL]
            onehot = (rows == names).astype(jnp.float32).astype(jnp.bfloat16)
            both = jnp.concatenate(split(ref[at : at + LOCAL, :]), axis=1)
            column = column + mul(onehot, both, NN)
    right[:, :COLUMNS], right[:, COLUMNS:] = split(column[:, :COLUMNS] + column[:, COLUMNS:])
    chunk = nx * OWNED
    per_step = TILE // chunk
    x_pos = x_ref[0]
    high_copy.wait()
    low_copy.wait()

    @pl.loop(0, nz // per_step)
    def _(step):
        at = tile_at(step)
        out = mul(high_ref[at, :], right[...], NN)
        scratch[...] = out[:, :COLUMNS] + (
            out[:, COLUMNS:] + mul(low_ref[at, :], right[:, :COLUMNS], NN)
        )
        for i in range(per_step):
            for k in range(nx):
                start = pl.multiple_of(i * chunk + (x_pos ^ k) * OWNED, OWNED)
                to = pl.multiple_of((step * per_step + i) * OWNED, OWNED)
                outs[k][pl.ds(to, OWNED), :] = scratch[pl.ds(start, OWNED), :]


def coarse_call(x_pos, half, other, high, low, n_grp, nz, nx):
    return call(
        functools.partial(coarse_kernel, n_grp, nz, nx),
        "coarse",
        [shaped(nz * OWNED, COLUMNS)] * nx,
        600 << 20,
        3 << 20,
        [SMEM] + [VMEM] * 2 + [HBM] * 2,
        scratch=[
            pltpu.VMEM((TILE, COLUMNS), jnp.float32),
            pltpu.VMEM((n_grp * OWNED, 2 * COLUMNS), jnp.bfloat16),
            pltpu.VMEM(high.shape, high.dtype),
            pltpu.VMEM(low.shape, low.dtype),
            pltpu.SemaphoreType.DMA((2,)),
        ],
    )(x_pos, half, other, high, low)


def add_kernel(*refs):
    count = len(refs) - 3
    out_ref, staged, sem = refs[count:]
    value = refs[0][...]
    for ref in refs[1:count]:
        value = value + ref[...]
    staged[...] = value
    fetched(staged, out_ref, sem).wait()


def add_call(*values):
    shape = values[0].shape
    (out,) = call(
        add_kernel,
        "add",
        [in_hbm(*shape)],
        1 << 20,
        1 << 20,
        [VMEM] * len(values),
        scratch=[pltpu.VMEM(shape, jnp.float32), pltpu.SemaphoreType.DMA],
    )(*values)
    return out


def sum_kernel(count, value_ref, out_ref):
    value = value_ref[:OWNED]
    for i in range(1, count):
        value = value + value_ref[i * OWNED : (i + 1) * OWNED]
    out_ref[...] = value


def sum_call(value):
    (out,) = call(
        functools.partial(sum_kernel, value.shape[0] // OWNED),
        "sum",
        [shaped(OWNED, COLUMNS)],
        1 << 20,
        1 << 18,
        [VMEM],
    )(value)
    return out


def fetch_kernel(n_grp, at_ref, map_ref, names_ref, half_ref, other_ref, *outs):
    dofs = n_grp * OWNED
    index = lax.broadcasted_iota(jnp.int32, (dofs, LOCAL), 0)
    block, inside = index // OWNED, index % OWNED
    block = jnp.where(block < n_grp // 2, 2 * block, 2 * block - n_grp + 1)
    ids = ((block ^ at_ref[0]) * OWNED + inside).astype(jnp.float32)
    value = jnp.concatenate([half_ref[...], other_ref[...]], axis=0)
    both = jnp.concatenate(split(value), axis=1)
    start = pl.multiple_of(at_ref[1] * TERM_ROWS + LOCAL, 8)
    names = [
        map_ref[:1, :LOCAL],
        names_ref[LOCAL : LOCAL + 1, :LOCAL],
        names_ref[pl.ds(start, 8), :][:1, :LOCAL],
    ]
    for name, out in zip(names, outs):
        onehot = (ids == name).astype(jnp.float32).astype(jnp.bfloat16)
        pair = mul(onehot, both, TN)
        out[...] = pair[:, :COLUMNS] + pair[:, COLUMNS:]


def fetch_call(at, map_row, names, half, other, n_grp):
    return call(
        functools.partial(fetch_kernel, n_grp),
        "fetch",
        [shaped(LOCAL, COLUMNS)] * 3,
        100 << 20,
        1 << 20,
        [SMEM] + [VMEM] * 4,
    )(at, map_row, names, half, other)


def matrix_copy(matrix_in, matrix, sems, t):
    at = tile_at(t)
    return pltpu.make_async_copy(matrix_in.at[:, at], matrix.at[:, at], sems.at[t])


def start_matrix(matrix_in, matrix, sems):
    for t in range(STEPS):
        matrix_copy(matrix_in, matrix, sems, t).start()


def apply(onehot_ref, matrix_in, matrix, sems, value_ref, rows_ref, result_ref):
    @pl.loop(0, STEPS)
    def _(t):
        put(rows_ref, tile_at(t), folded(mul(value_ref[...], onehot_ref[tile_at(t), :], NT)))

    @pl.loop(0, STEPS)
    def _(t):
        matrix_copy(matrix_in, matrix, sems, t).wait()
        high, low = split(matrix[:, tile_at(t)])
        out = folded(mul(rows_ref[...], high, NN)) + mul(rows_ref[:COLUMNS], low, NN)
        put(result_ref, tile_at(t), out)


MATRIX = [
    pltpu.VMEM((INTERFACE, INTERFACE), jnp.float32),
    pltpu.SemaphoreType.DMA((STEPS,)),
]


def local_kernel(first, onehot_ref, weighted_in, matrix_in, weight_ref, lift_in, *rest):
    outs = rest[:FACES]
    matrix, matrix_sems, weighted, lift, sems, rows, result, staged = rest[FACES:]
    weighted_copy = fetched(weighted_in, weighted, sems.at[0])
    start_matrix(matrix_in, matrix, matrix_sems)
    lift_copy = fetched(lift_in, lift, sems.at[1])
    weighted_copy.wait()
    apply(onehot_ref, matrix_in, matrix, matrix_sems, weighted, rows, result)
    lift_copy.wait()
    copies = []
    for p in range(FACES):
        out = folded(mul(result[...], onehot_ref[:, face_at(p)], NN))
        staged[p, :COLUMNS] = weight_ref[:1, face_at(p)] * out
        if first:
            staged[p, COLUMNS:] = lift[:, face_at(p)]
        copies.append(fetched(staged.at[p], outs[p], sems.at[2 + p]))
    for copy in copies:
        copy.wait()


def local_call(onehot, weighted, matrix, weight, lift, first):
    rows = LIFT_ROWS if first else COLUMNS
    return call(
        functools.partial(local_kernel, first),
        "local",
        [in_hbm(rows, FACE_ROWS)] * FACES,
        6 << 30,
        8 << 20,
        [VMEM, HBM, HBM, VMEM, HBM],
        scratch=MATRIX
        + [PAIR, pltpu.VMEM((LOCAL, INTERFACE), jnp.float32), pltpu.SemaphoreType.DMA((6,))]
        + [PAIR] * 2
        + [pltpu.VMEM((FACES, rows, FACE_ROWS), jnp.float32)],
    )(onehot, weighted, matrix, weight, lift)


BODY = slice(0, COLUMNS)
LIFT = slice(COLUMNS, LIFT_ROWS)


def adjoint_face(p, near, far, lift_near, lift_far, own, around):
    change = mul3(own, split(lift_near), TN)
    change = change + mul3(split(around[p][...]), split(lift_far), TN)
    return near + far + change


def middle_kernel(onehot_ref, *refs):
    groups = [refs[i * FACES : (i + 1) * FACES] for i in range(4)]
    near_in, far_in, around, gradient_in = groups
    own_ref, matrix_in, adjoint_out = refs[4 * FACES : 4 * FACES + 3]
    outs = refs[4 * FACES + 3 : 5 * FACES + 3]
    matrix, matrix_sems, near, far, gradient, sems, kept, value, rows, result = refs[
        5 * FACES + 3 :
    ]
    copies = [
        (fetched(near_in[p], near.at[p], sems.at[0, p]), fetched(far_in[p], far.at[p], sems.at[1, p]))
        for p in range(FACES)
    ]
    start_matrix(matrix_in, matrix, matrix_sems)
    gradient_copies = [
        fetched(gradient_in[p], gradient.at[p], sems.at[2, p]) for p in range(FACES)
    ]
    own = split(own_ref[...])
    kept_copies = []
    for p in range(FACES):
        for copy in copies[p]:
            copy.wait()
        adjoint = adjoint_face(
            p, near[p, BODY], far[p, BODY], near[p, LIFT], far[p, LIFT], own, around
        )
        kept[p] = adjoint
        kept_copies.append(fetched(kept.at[p], adjoint_out.at[p], sems.at[3, p]))
        put(value, face_at(p), adjoint)
    apply(onehot_ref, matrix_in, matrix, matrix_sems, value, rows, result)
    for p in range(FACES):
        gradient_copies[p].wait()
        out = folded(mul(result[...], onehot_ref[:, face_at(p)], NN))
        outs[p][:COLUMNS] = gradient[p, BODY] - out
        outs[p][COLUMNS:] = gradient[p, COLUMNS:]
    for copy in kept_copies:
        copy.wait()


def middle_call(onehot, near, far, around, gradient, own, matrix):
    lifted = pltpu.VMEM((FACES, LIFT_ROWS, FACE_ROWS), jnp.float32)
    return call(
        middle_kernel,
        "middle",
        [in_hbm(FACES, COLUMNS, FACE_ROWS)] + [shaped(MULT_ROWS, FACE_ROWS)] * FACES,
        6 << 30,
        12 << 20,
        [VMEM] + [HBM] * (2 * FACES) + [VMEM] * FACES + [HBM] * FACES + [VMEM, HBM],
        scratch=MATRIX
        + [
            lifted,
            lifted,
            pltpu.VMEM((FACES, MULT_ROWS, FACE_ROWS), jnp.float32),
            pltpu.SemaphoreType.DMA((4, FACES)),
            pltpu.VMEM((FACES, COLUMNS, FACE_ROWS), jnp.float32),
        ]
        + [PAIR] * 3,
    )(onehot, *near, *far, *around, *gradient, own, matrix)


def last_kernel(onehot_ref, *refs):
    groups = [refs[i * FACES : (i + 1) * FACES] for i in range(5)]
    near_in, far_in, lift_near_in, lift_far_in, around = groups
    own_ref, adjoint_in, out_ref = refs[5 * FACES : 5 * FACES + 3]
    near, far, adjoint, lift_near, lift_far, sems, value, staged, out_sems = refs[5 * FACES + 3 :]
    copies = []
    for p in range(FACES):
        pieces = (
            (near_in[p], near.at[p]),
            (far_in[p], far.at[p]),
            (adjoint_in.at[p], adjoint.at[p]),
            (lift_near_in[p].at[LIFT], lift_near.at[p]),
            (lift_far_in[p].at[LIFT], lift_far.at[p]),
        )
        copies.append(
            [fetched(source, to, sems.at[i, p]) for i, (source, to) in enumerate(pieces)]
        )
    own = split(own_ref[...])
    for p in range(FACES):
        for copy in copies[p]:
            copy.wait()
        out = adjoint_face(p, near[p], far[p], lift_near[p], lift_far[p], own, around)
        put(value, face_at(p), adjoint[p] + out)
    out_copies = []
    for t in range(STEPS):
        at = slice(t * TILE, (t + 1) * TILE)
        out = mul(onehot_ref[at, :], value[...], NT)
        staged[t] = out[:, :COLUMNS] + out[:, COLUMNS:]
        out_copies.append(fetched(staged.at[t], out_ref.at[at], out_sems.at[t]))
    for copy in out_copies:
        copy.wait()


def last_call(onehot, near, far, lift_near, lift_far, around, own, adjoint):
    face_block = pltpu.VMEM((FACES, COLUMNS, FACE_ROWS), jnp.float32)
    lift_block = pltpu.VMEM((FACES, LOCAL, FACE_ROWS), jnp.float32)
    (out,) = call(
        last_kernel,
        "last",
        [in_hbm(INTERFACE, COLUMNS)],
        1 << 30,
        6 << 20,
        [VMEM] + [HBM] * (4 * FACES) + [VMEM] * FACES + [VMEM, HBM],
        scratch=[
            face_block,
            face_block,
            face_block,
            lift_block,
            lift_block,
            pltpu.SemaphoreType.DMA((5, FACES)),
            PAIR,
            pltpu.VMEM((STEPS, TILE, COLUMNS), jnp.float32),
            pltpu.SemaphoreType.DMA((STEPS,)),
        ],
    )(onehot, *near, *far, *lift_near, *lift_far, *around, own, adjoint)
    return out


def on_device(
    objective, schur, local_inverse, coarse_basis, coarse_inverse, stiffness, face_rows, coarse_map
):
    n_grp, n_dev = lax.axis_size("grp"), lax.axis_size("dev")
    nx = X_SIZE
    nz = n_dev // nx
    grp = lax.axis_index("grp").astype(jnp.int32)
    dev = lax.axis_index("dev").astype(jnp.int32)
    x_pos = (dev % nx).reshape(1)
    z_groups = [[z * nx + x for z in range(nz)] for x in range(nx)]
    odd = jnp.stack([dev % 2, grp % 2])
    beyond = jnp.where(grp % 2 == 1, grp + 1, grp - 1)
    beyond = jnp.where((beyond < 0) | (beyond >= n_grp), grp ^ 1, beyond)
    at = jnp.stack([grp, (grp ^ beyond) // 2])

    def swap(value, axis, k):
        size = lax.axis_size(axis)
        return lax.ppermute(value, axis, [(i, i ^ k) for i in range(size)])

    def swap_next(value, axis):
        lower = range(1, lax.axis_size(axis) - 1, 2)
        return lax.ppermute(
            value, axis, [(i, i + 1) for i in lower] + [(i + 1, i) for i in lower]
        )

    def group_gather(value):
        parts = [value] + [swap(value, "grp", k) for k in range(2, n_grp, 2)]
        half = join_call(parts)
        return half, swap(half, "grp", 1)

    def exchange(faces):
        return [
            swap(faces[0], "dev", 1),
            swap_next(faces[1], "dev"),
            swap(faces[2], "grp", 1),
            swap_next(faces[3], "grp"),
        ]

    local_map = coarse_map[0, 0]
    basis, onehot, *gradient = pack_call(
        odd, face_rows[0, 0], objective[0, 0], coarse_basis[0, 0], stiffness[0]
    )
    tile, *gradient = lax.optimization_barrier((coarse_inverse, *gradient))
    high, low = tile_call(tile.reshape(-1, tile.shape[3]))
    arrived = exchange(gradient)

    map_row = jnp.zeros((8, COLUMNS), jnp.float32)
    map_row = map_row.at[0, :LOCAL].set(local_map.astype(jnp.float32))
    high, low, map_row = lax.optimization_barrier((high, low, map_row))

    weighted, terms, weight, lift = weigh_call(gradient, arrived, basis, map_row, True)
    names = None
    adjoint = None
    lift_near = lift_far = None
    for sweep in range(SWEEPS):
        first = sweep == 0
        half, other = group_gather(terms)
        if first:
            names = other
        blocks = coarse_call(x_pos, half, other, high, low, n_grp, nz, nx)
        sent = [swap(blocks[k], "dev", k) for k in (2, 1, 3)]
        near = local_call(onehot, weighted, local_inverse[0, 0], weight, lift, first)
        mine, *near = lax.optimization_barrier((blocks[0], *near))
        total = add_call(mine, *sent)
        total = lax.all_to_all(
            total.reshape(nz, OWNED, COLUMNS), "dev", 0, 0, axis_index_groups=z_groups, tiled=True
        )
        far = exchange(near)
        total, *far = lax.optimization_barrier((total, *far))
        owned = sum_call(total.reshape(nz * OWNED, COLUMNS))
        if first:
            lift_near, lift_far = near, far
        own, core, next_core = fetch_call(at, map_row, names, *group_gather(owned), n_grp)
        around = [swap(own, "dev", 1), swap_next(own, "dev"), core, next_core]
        if first:
            adjoint, *remain = middle_call(onehot, near, far, around, gradient, own, schur[0, 0])
            weighted, terms = weigh_call(remain, exchange(remain), basis, map_row, False)
        else:
            out = last_call(onehot, near, far, lift_near, lift_far, around, own, adjoint)
    return out[None, None]


def solution(mesh):
    return jax.shard_map(
        on_device,
        mesh=mesh,
        in_specs=(
            P("grp", "dev", None, None),
            P("grp", "dev", None, None),
            P("grp", "dev", None, None),
            P("grp", "dev", None, None),
            P(None, "dev", None, "grp"),
            P("grp", "dev", None),
            P("grp", "dev", None, None),
            P("grp", "dev", None),
        ),
        out_specs=P("grp", "dev", None, None),
        check_vma=False,
    )
```

```python
import functools

import jax
import jax.numpy as jnp
from jax import lax
from jax.experimental import pallas as pl
from jax.experimental.pallas import tpu as pltpu
from jax.sharding import PartitionSpec as P

INTERFACE = 1024
FACE_ROWS = 256
COLUMNS = 256
OWNED = 32
SPLIT = False
LOCAL = 64
SWEEPS = 2
X_SIZE = 4
TILE = 256
FACES = 4
TERM_ROWS = LOCAL + 8
MULT_ROWS = COLUMNS + 8
LIFT_ROWS = COLUMNS + LOCAL

NN = (((1,), (0,)), ((), ()))
NT = (((1,), (1,)), ((), ()))
TN = (((0,), (0,)), ((), ()))

VMEM = pl.BlockSpec(memory_space=pltpu.VMEM)
SMEM = pl.BlockSpec(memory_space=pltpu.SMEM)
ANY = pl.BlockSpec(memory_space=pl.ANY)
HBM = "hbm"


def shaped(*shape, dtype=jnp.float32):
    return jax.ShapeDtypeStruct(shape, dtype)


def in_hbm(*shape, dtype=jnp.float32):
    return pltpu.HBM(shape, dtype)


def params():
    return pltpu.CompilerParams(vmem_limit_bytes=20 << 20)


def cost(flops, moved):
    return pl.CostEstimate(flops=flops, bytes_accessed=moved, transcendentals=0)


def call(kernel, name, out_shape, flops, moved, in_specs, scratch=()):
    outs = [VMEM if isinstance(o, jax.ShapeDtypeStruct) else ANY for o in out_shape]
    function = pl.pallas_call(
        kernel,
        out_shape=out_shape,
        in_specs=[ANY if spec is HBM else spec for spec in in_specs],
        out_specs=outs,
        scratch_shapes=scratch,
        compiler_params=params(),
        cost_estimate=cost(flops, moved),
        name=name,
    )

    def run(*values):
        values = [
            pltpu.with_memory_space_constraint(value, pltpu.HBM) if spec is HBM else value
            for value, spec in zip(values, in_specs)
        ]
        return function(*values)

    return run


def split(value):
    high = value.astype(jnp.bfloat16)
    low = (value - high.astype(jnp.float32)).astype(jnp.bfloat16)
    return high, low


def mul(left, right, dims):
    return lax.dot_general(left, right, dims, preferred_element_type=jnp.float32)


def mul3(left, right, dims):
    left_high, left_low = left
    right_high, right_low = right
    return (
        mul(left_high, right_low, dims)
        + mul(left_low, right_high, dims)
        + mul(left_high, right_high, dims)
    )


def folded(value):
    return value[:COLUMNS] + value[COLUMNS:]


def tile_at(t):
    return pl.ds(pl.multiple_of(t * TILE, TILE), TILE)


def face_at(p):
    return slice(p * FACE_ROWS, (p + 1) * FACE_ROWS)


def put(ref, at, value):
    ref[:COLUMNS, at], ref[COLUMNS:, at] = split(value)


PAIR = pltpu.VMEM((2 * COLUMNS, INTERFACE), jnp.bfloat16)
STEPS = INTERFACE // TILE
BASIS_AT = 2 * COLUMNS
MULT_AT = BASIS_AT + 2 * LOCAL


def fetched(source, target, sem):
    copy = pltpu.make_async_copy(source, target, sem)
    copy.start()
    return copy


def pack_kernel(
    odd_ref, slots_in, objective_in, basis_in, mult_in, basis_ref, onehot_ref, *rest
):
    outs = rest[:FACES]
    slots, staged, basis, mult, sems, left = rest[FACES:]
    slots_copy = fetched(slots_in, slots, sems.at[STEPS])
    small = [
        fetched(basis_in, basis, sems.at[STEPS + 1]),
        fetched(mult_in, mult, sems.at[STEPS + 2]),
    ]
    copies = [
        fetched(objective_in.at[t * TILE : (t + 1) * TILE], staged.at[t], sems.at[t])
        for t in range(STEPS)
    ]
    slots_copy.wait()
    odd_dev, odd_grp = odd_ref[0] == 1, odd_ref[1] == 1
    lines = [slots[p : p + 1] for p in range(FACES)]
    lines = [
        jnp.where(odd_dev, lines[0], lines[1]),
        jnp.where(odd_dev, lines[1], lines[0]),
        jnp.where(odd_grp, lines[2], lines[3]),
        jnp.where(odd_grp, lines[3], lines[2]),
    ]
    for p in range(FACES):
        rows = lax.broadcasted_iota(jnp.int32, (INTERFACE, FACE_ROWS), 0)
        onehot_ref[:, face_at(p)] = (
            (rows == lines[p]).astype(jnp.float32).astype(jnp.bfloat16)
        )
    for copy in small:
        copy.wait()
    left[BASIS_AT : BASIS_AT + LOCAL], left[BASIS_AT + LOCAL : MULT_AT] = split(basis[...])
    left[MULT_AT:] = jnp.broadcast_to(mult[...].astype(jnp.float32), (16, INTERFACE)).astype(
        jnp.bfloat16
    )
    for t in range(STEPS):
        copies[t].wait()
        at = slice(t * TILE, (t + 1) * TILE)
        left[:COLUMNS, at], left[COLUMNS:BASIS_AT, at] = split(staged[t].T)
    for p in range(FACES):
        out = mul(left[...], onehot_ref[:, face_at(p)], NN)
        outs[p][:COLUMNS] = folded(out[:BASIS_AT])
        outs[p][COLUMNS:] = out[MULT_AT : MULT_AT + 8]
        basis_ref[:, face_at(p)] = out[BASIS_AT : BASIS_AT + LOCAL] + out[BASIS_AT + LOCAL : MULT_AT]


def pack_call(odd, slots, objective, basis, mult):
    return call(
        pack_kernel,
        "pack",
        [shaped(LOCAL, INTERFACE), shaped(INTERFACE, INTERFACE, dtype=jnp.bfloat16)]
        + [shaped(MULT_ROWS, FACE_ROWS)] * FACES,
        2 << 30,
        4 << 20,
        [SMEM] + [HBM] * 4,
        scratch=[
            pltpu.VMEM((FACES, FACE_ROWS), jnp.int32),
            pltpu.VMEM((STEPS, TILE, COLUMNS), jnp.float32),
            pltpu.VMEM((LOCAL, INTERFACE), jnp.float32),
            pltpu.VMEM((1, INTERFACE), jnp.int32),
            pltpu.SemaphoreType.DMA((STEPS + 3,)),
            pltpu.VMEM((MULT_AT + 16, INTERFACE), jnp.bfloat16),
        ],
    )(odd, slots, objective, basis, mult)


def tile_kernel(tile_in, high_out, low_out, staged, sems, high, low, out_sems):
    copies = [
        fetched(tile_in.at[:, t * TILE : (t + 1) * TILE], staged.at[t], sems.at[t])
        for t in range(STEPS)
    ]
    outs = []
    for t in range(STEPS):
        copies[t].wait()
        at = slice(t * TILE, (t + 1) * TILE)
        high[at], low[at] = split(staged[t].T)
        outs.append(fetched(high.at[at], high_out.at[at], out_sems.at[0, t]))
        outs.append(fetched(low.at[at], low_out.at[at], out_sems.at[1, t]))
    for copy in outs:
        copy.wait()


def tile_call(tile):
    rows, width = tile.shape
    half = pltpu.VMEM((width, rows), jnp.bfloat16)
    return call(
        tile_kernel,
        "tile",
        [in_hbm(width, rows, dtype=jnp.bfloat16)] * 2,
        1 << 20,
        4 << 20,
        [HBM],
        scratch=[
            pltpu.VMEM((STEPS, rows, TILE), jnp.float32),
            pltpu.SemaphoreType.DMA((STEPS,)),
            half,
            half,
            pltpu.SemaphoreType.DMA((2, STEPS)),
        ],
    )(tile)


def join_kernel(*refs):
    rows = refs[0].shape[0]
    for i, ref in enumerate(refs[:-1]):
        refs[-1][i * rows : (i + 1) * rows] = ref[...]


def join_call(parts):
    rows, width = parts[0].shape
    (out,) = call(
        join_kernel,
        "join",
        [shaped(len(parts) * rows, width)],
        1 << 20,
        1 << 19,
        [VMEM] * len(parts),
    )(*parts)
    return out


def weigh_kernel(first, *refs):
    here, there = refs[:FACES], refs[FACES : 2 * FACES]
    basis_ref, map_ref = refs[2 * FACES : 2 * FACES + 2]
    weighted_out, terms_ref = refs[2 * FACES + 2 : 2 * FACES + 4]
    if first:
        weight_ref, lift_out, weighted_ref, sems, lift_ref = refs[2 * FACES + 4 :]
    else:
        weighted_ref, sems = refs[2 * FACES + 4 :]
    copies = []
    for p in range(FACES):
        mine = here[p][COLUMNS : COLUMNS + 1]
        total = mine + there[p][COLUMNS : COLUMNS + 1]
        weight = jnp.where(total > 0, mine / jnp.maximum(total, 1.0), 0.0)
        put(weighted_ref, face_at(p), weight * (here[p][:COLUMNS] + there[p][:COLUMNS]))
        at = (slice(None), face_at(p))
        copies.append(fetched(weighted_ref.at[at], weighted_out.at[at], sems.at[p]))
        if first:
            weight_ref[:, face_at(p)] = jnp.broadcast_to(weight, (8, FACE_ROWS))
            lift_ref[:, face_at(p)] = basis_ref[:, face_at(p)] * weight
            copies.append(fetched(lift_ref.at[at], lift_out.at[at], sems.at[FACES + p]))
    terms = jnp.zeros((LOCAL, COLUMNS), jnp.float32)
    for p in range(FACES):
        right = (weighted_ref[:COLUMNS, face_at(p)], weighted_ref[COLUMNS:, face_at(p)])
        terms = terms + mul3(split(basis_ref[:, face_at(p)]), right, NT)
    terms_ref[:LOCAL] = terms
    terms_ref[LOCAL:] = map_ref[...]
    for copy in copies:
        copy.wait()


def weigh_call(here, there, basis, map_row, first):
    out = [in_hbm(2 * COLUMNS, INTERFACE, dtype=jnp.bfloat16), shaped(TERM_ROWS, COLUMNS)]
    scratch = [PAIR, pltpu.SemaphoreType.DMA((2 * FACES,))]
    if first:
        out += [shaped(8, INTERFACE), in_hbm(LOCAL, INTERFACE)]
        scratch += [pltpu.VMEM((LOCAL, INTERFACE), jnp.float32)]
    return call(
        functools.partial(weigh_kernel, first),
        "weigh",
        out,
        100 << 20,
        2 << 20,
        [VMEM] * (2 * FACES + 2),
        scratch=scratch,
    )(*here, *there, basis, map_row)


def coarse_kernel(n_grp, nz, nx, x_ref, half_ref, other_ref, high_in, low_in, *rest):
    outs, (scratch, right, high_ref, low_ref, sems) = rest[:nx], rest[nx:]

    def pieces(step):
        at = tile_at(step)
        return (
            pltpu.make_async_copy(high_in.at[at], high_ref.at[at], sems.at[0, step]),
            pltpu.make_async_copy(low_in.at[at], low_ref.at[at], sems.at[1, step]),
        )

    for step in range(STEPS):
        for copy in pieces(step):
            copy.start()
    dofs = n_grp * OWNED
    column = jnp.zeros((dofs, 2 * COLUMNS), jnp.float32)
    rows = lax.broadcasted_iota(jnp.int32, (dofs, LOCAL), 0).astype(jnp.float32)
    for ref in (half_ref, other_ref):
        for j in range(n_grp // 2):
            at = j * TERM_ROWS
            names = ref[at + LOCAL : at + LOCAL + 1, :LOCAL]
            onehot = (rows == names).astype(jnp.float32).astype(jnp.bfloat16)
            both = jnp.concatenate(split(ref[at : at + LOCAL, :]), axis=1)
            column = column + mul(onehot, both, NN)
    right[:, :COLUMNS], right[:, COLUMNS:] = split(column[:, :COLUMNS] + column[:, COLUMNS:])
    chunk = nx * OWNED
    per_step = TILE // chunk
    x_pos = x_ref[0]

    @pl.loop(0, nz // per_step)
    def _(step):
        at = tile_at(step)
        for copy in pieces(step):
            copy.wait()
        out = mul(high_ref[at, :], right[...], NN)
        scratch[...] = out[:, :COLUMNS] + (
            out[:, COLUMNS:] + mul(low_ref[at, :], right[:, :COLUMNS], NN)
        )
        for i in range(per_step):
            for k in range(nx):
                start = pl.multiple_of(i * chunk + (x_pos ^ k) * OWNED, OWNED)
                to = pl.multiple_of((step * per_step + i) * OWNED, OWNED)
                outs[k][pl.ds(to, OWNED), :] = scratch[pl.ds(start, OWNED), :]


def coarse_call(x_pos, half, other, high, low, n_grp, nz, nx):
    return call(
        functools.partial(coarse_kernel, n_grp, nz, nx),
        "coarse",
        [shaped(nz * OWNED, COLUMNS)] * nx,
        600 << 20,
        3 << 20,
        [SMEM] + [VMEM] * 2 + [HBM] * 2,
        scratch=[
            pltpu.VMEM((TILE, COLUMNS), jnp.float32),
            pltpu.VMEM((n_grp * OWNED, 2 * COLUMNS), jnp.bfloat16),
            pltpu.VMEM(high.shape, high.dtype),
            pltpu.VMEM(low.shape, low.dtype),
            pltpu.SemaphoreType.DMA((2, STEPS)),
        ],
    )(x_pos, half, other, high, low)


def add_kernel(*refs):
    count = len(refs) - 3
    out_ref, staged, sem = refs[count:]
    value = refs[0][...]
    for ref in refs[1:count]:
        value = value + ref[...]
    staged[...] = value
    fetched(staged, out_ref, sem).wait()


def add_call(*values):
    shape = values[0].shape
    (out,) = call(
        add_kernel,
        "add",
        [in_hbm(*shape)],
        1 << 20,
        1 << 20,
        [VMEM] * len(values),
        scratch=[pltpu.VMEM(shape, jnp.float32), pltpu.SemaphoreType.DMA],
    )(*values)
    return out


def sum_kernel(count, value_ref, out_ref):
    value = value_ref[:OWNED]
    for i in range(1, count):
        value = value + value_ref[i * OWNED : (i + 1) * OWNED]
    out_ref[...] = value


def sum_call(value):
    (out,) = call(
        functools.partial(sum_kernel, value.shape[0] // OWNED),
        "sum",
        [shaped(OWNED, COLUMNS)],
        1 << 20,
        1 << 18,
        [VMEM],
    )(value)
    return out


def fetch_kernel(n_grp, at_ref, map_ref, names_ref, half_ref, other_ref, *outs):
    dofs = n_grp * OWNED
    index = lax.broadcasted_iota(jnp.int32, (dofs, LOCAL), 0)
    block, inside = index // OWNED, index % OWNED
    block = jnp.where(block < n_grp // 2, 2 * block, 2 * block - n_grp + 1)
    ids = ((block ^ at_ref[0]) * OWNED + inside).astype(jnp.float32)
    value = jnp.concatenate([half_ref[...], other_ref[...]], axis=0)
    both = jnp.concatenate(split(value), axis=1)
    start = pl.multiple_of(at_ref[1] * TERM_ROWS + LOCAL, 8)
    names = [
        map_ref[:1, :LOCAL],
        names_ref[LOCAL : LOCAL + 1, :LOCAL],
        names_ref[pl.ds(start, 8), :][:1, :LOCAL],
    ]
    for name, out in zip(names, outs):
        onehot = (ids == name).astype(jnp.float32).astype(jnp.bfloat16)
        pair = mul(onehot, both, TN)
        out[...] = pair[:, :COLUMNS] + pair[:, COLUMNS:]


def fetch_call(at, map_row, names, half, other, n_grp):
    return call(
        functools.partial(fetch_kernel, n_grp),
        "fetch",
        [shaped(LOCAL, COLUMNS)] * 3,
        100 << 20,
        1 << 20,
        [SMEM] + [VMEM] * 4,
    )(at, map_row, names, half, other)


def matrix_copy(matrix_in, matrix, sems, t):
    at = tile_at(t)
    return pltpu.make_async_copy(matrix_in.at[:, at], matrix.at[:, at], sems.at[t])


def start_matrix(matrix_in, matrix, sems, tiles):
    for t in tiles:
        matrix_copy(matrix_in, matrix, sems, t).start()


def to_rows(onehot_ref, value_ref, rows_ref):
    @pl.loop(0, STEPS)
    def _(t):
        put(rows_ref, tile_at(t), folded(mul(value_ref[...], onehot_ref[tile_at(t), :], NT)))


def product(rows_ref, high, low):
    return folded(mul(rows_ref[...], high, NN)) + mul(rows_ref[:COLUMNS], low, NN)


MATRIX = [
    pltpu.VMEM((INTERFACE, INTERFACE), jnp.float32),
    pltpu.SemaphoreType.DMA((STEPS,)),
]


def local_kernel(first, onehot_ref, weighted_in, matrix_in, weight_ref, lift_in, *rest):
    outs = rest[:FACES]
    matrix, matrix_sems, weighted, lift, sems, rows, result, staged = rest[FACES:]
    weighted_copy = fetched(weighted_in, weighted, sems.at[0])
    start_matrix(matrix_in, matrix, matrix_sems, range(2))
    weighted_copy.wait()
    start_matrix(matrix_in, matrix, matrix_sems, range(2, STEPS))
    lift_copy = fetched(lift_in, lift, sems.at[1])
    to_rows(onehot_ref, weighted, rows)

    @pl.loop(0, STEPS)
    def _(t):
        matrix_copy(matrix_in, matrix, matrix_sems, t).wait()
        put(result, tile_at(t), product(rows, *split(matrix[:, tile_at(t)])))

    lift_copy.wait()
    copies = []
    for p in range(FACES):
        out = folded(mul(result[...], onehot_ref[:, face_at(p)], NN))
        staged[p, :COLUMNS] = weight_ref[:1, face_at(p)] * out
        if first:
            staged[p, COLUMNS:] = lift[:, face_at(p)]
        copies.append(fetched(staged.at[p], outs[p], sems.at[2 + p]))
    for copy in copies:
        copy.wait()


def local_call(onehot, weighted, matrix, weight, lift, first):
    rows = LIFT_ROWS if first else COLUMNS
    return call(
        functools.partial(local_kernel, first),
        "local",
        [in_hbm(rows, FACE_ROWS)] * FACES,
        6 << 30,
        8 << 20,
        [VMEM, HBM, HBM, VMEM, HBM],
        scratch=MATRIX
        + [PAIR, pltpu.VMEM((LOCAL, INTERFACE), jnp.float32), pltpu.SemaphoreType.DMA((6,))]
        + [PAIR] * 2
        + [pltpu.VMEM((FACES, rows, FACE_ROWS), jnp.float32)],
    )(onehot, weighted, matrix, weight, lift)


BODY = slice(0, COLUMNS)
LIFT = slice(COLUMNS, LIFT_ROWS)
FACE_BLOCK = pltpu.VMEM((FACES, COLUMNS, FACE_ROWS), jnp.float32)


def lift_copies(near_in, far_in, lift_ref, sems):
    copies = []
    for p in range(FACES):
        copies.append(fetched(near_in[p].at[LIFT], lift_ref.at[p, :LOCAL], sems.at[0, p]))
        copies.append(fetched(far_in[p].at[LIFT], lift_ref.at[p, LOCAL:], sems.at[1, p]))
    return copies


def body_copies(near_in, far_in, near, far, sems):
    return [
        (
            fetched(near_in[p].at[BODY], near.at[p], sems.at[2, p]),
            fetched(far_in[p].at[BODY], far.at[p], sems.at[3, p]),
        )
        for p in range(FACES)
    ]


def ready_kernel(*refs):
    near_in, far_in, gradient_in = (refs[i * FACES : (i + 1) * FACES] for i in range(3))
    matrix_in, base_ref, lift_ref, gradient_ref, high_ref, low_ref = refs[
        3 * FACES : 3 * FACES + 6
    ]
    matrix, matrix_sems, near, far, sems = refs[3 * FACES + 6 :]
    bodies = body_copies(near_in, far_in, near, far, sems)
    start_matrix(matrix_in, matrix, matrix_sems, range(STEPS))
    copies = lift_copies(near_in, far_in, lift_ref, sems)
    for p in range(FACES):
        copies.append(fetched(gradient_in[p], gradient_ref.at[p], sems.at[4, p]))
    for p in range(FACES):
        for copy in bodies[p]:
            copy.wait()
        base_ref[p] = near[p] + far[p]

    @pl.loop(0, STEPS)
    def _(t):
        matrix_copy(matrix_in, matrix, matrix_sems, t).wait()
        high_ref[:, tile_at(t)], low_ref[:, tile_at(t)] = split(matrix[:, tile_at(t)])

    for copy in copies:
        copy.wait()


def ready_call(near, far, gradient, matrix):
    half = shaped(INTERFACE, INTERFACE, dtype=jnp.bfloat16)
    return call(
        ready_kernel,
        "ready",
        [
            shaped(FACES, COLUMNS, FACE_ROWS),
            shaped(FACES, 2 * LOCAL, FACE_ROWS),
            shaped(FACES, MULT_ROWS, FACE_ROWS),
            half,
            half,
        ],
        4 << 20,
        8 << 20,
        [HBM] * (3 * FACES + 1),
        scratch=MATRIX + [FACE_BLOCK, FACE_BLOCK, pltpu.SemaphoreType.DMA((5, FACES))],
    )(*near, *far, *gradient, matrix)


def ready_last_kernel(*refs):
    near_in, far_in, lift_near_in, lift_far_in = (
        refs[i * FACES : (i + 1) * FACES] for i in range(4)
    )
    adjoint_in, base_ref, lift_ref, near, far, adjoint, sems = refs[4 * FACES :]
    bodies = body_copies(near_in, far_in, near, far, sems)
    kept = [fetched(adjoint_in.at[p], adjoint.at[p], sems.at[4, p]) for p in range(FACES)]
    copies = lift_copies(lift_near_in, lift_far_in, lift_ref, sems)
    for p in range(FACES):
        for copy in bodies[p]:
            copy.wait()
        kept[p].wait()
        base_ref[p] = near[p] + far[p] + adjoint[p]
    for copy in copies:
        copy.wait()


def ready_last_call(near, far, lift_near, lift_far, adjoint):
    return call(
        ready_last_kernel,
        "ready_last",
        [shaped(FACES, COLUMNS, FACE_ROWS), shaped(FACES, 2 * LOCAL, FACE_ROWS)],
        4 << 20,
        5 << 20,
        [HBM] * (4 * FACES + 1),
        scratch=[FACE_BLOCK] * 3 + [pltpu.SemaphoreType.DMA((5, FACES))],
    )(*near, *far, *lift_near, *lift_far, adjoint)


def adjoint_face(base, lift, own, around):
    both = jnp.concatenate([own[...], around[...]], axis=0)
    return base + mul3(split(both), split(lift), TN)


def middle_kernel(onehot_ref, base_ref, lift_ref, gradient_ref, high_ref, low_ref, *refs):
    around, own_ref, adjoint_out = refs[:FACES], refs[FACES], refs[FACES + 1]
    outs, (sems, kept, value, rows, result) = refs[FACES + 2 : 2 * FACES + 2], refs[2 * FACES + 2 :]
    copies = []
    for p in range(FACES):
        adjoint = adjoint_face(base_ref[p], lift_ref[p], own_ref, around[p])
        kept[p] = adjoint
        copies.append(fetched(kept.at[p], adjoint_out.at[p], sems.at[p]))
        put(value, face_at(p), adjoint)
    to_rows(onehot_ref, value, rows)

    @pl.loop(0, STEPS)
    def _(t):
        put(result, tile_at(t), product(rows, high_ref[:, tile_at(t)], low_ref[:, tile_at(t)]))

    for p in range(FACES):
        out = folded(mul(result[...], onehot_ref[:, face_at(p)], NN))
        outs[p][:COLUMNS] = gradient_ref[p, BODY] - out
        outs[p][COLUMNS:] = gradient_ref[p, COLUMNS:]
    for copy in copies:
        copy.wait()


def middle_call(onehot, ready, around, own):
    return call(
        middle_kernel,
        "middle",
        [in_hbm(FACES, COLUMNS, FACE_ROWS)] + [shaped(MULT_ROWS, FACE_ROWS)] * FACES,
        6 << 30,
        12 << 20,
        [VMEM] * (7 + FACES),
        scratch=[pltpu.SemaphoreType.DMA((FACES,)), FACE_BLOCK] + [PAIR] * 3,
    )(onehot, *ready, *around, own)


def last_kernel(onehot_ref, base_ref, lift_ref, *refs):
    around, (own_ref, out_ref, value, staged, sems) = refs[:FACES], refs[FACES:]
    for p in range(FACES):
        put(value, face_at(p), adjoint_face(base_ref[p], lift_ref[p], own_ref, around[p]))
    copies = []
    for t in range(STEPS):
        at = slice(t * TILE, (t + 1) * TILE)
        out = mul(onehot_ref[at, :], value[...], NT)
        staged[t] = out[:, :COLUMNS] + out[:, COLUMNS:]
        copies.append(fetched(staged.at[t], out_ref.at[at], sems.at[t]))
    for copy in copies:
        copy.wait()


def last_call(onehot, ready, around, own):
    (out,) = call(
        last_kernel,
        "last",
        [in_hbm(INTERFACE, COLUMNS)],
        1 << 30,
        6 << 20,
        [VMEM] * (4 + FACES),
        scratch=[
            PAIR,
            pltpu.VMEM((STEPS, TILE, COLUMNS), jnp.float32),
            pltpu.SemaphoreType.DMA((STEPS,)),
        ],
    )(onehot, *ready, *around, own)
    return out


def on_device(
    objective, schur, local_inverse, coarse_basis, coarse_inverse, stiffness, face_rows, coarse_map
):
    n_grp, n_dev = lax.axis_size("grp"), lax.axis_size("dev")
    nx = X_SIZE
    nz = n_dev // nx
    grp = lax.axis_index("grp").astype(jnp.int32)
    dev = lax.axis_index("dev").astype(jnp.int32)
    x_pos = (dev % nx).reshape(1)
    z_groups = [[z * nx + x for z in range(nz)] for x in range(nx)]
    odd = jnp.stack([dev % 2, grp % 2])
    beyond = jnp.where(grp % 2 == 1, grp + 1, grp - 1)
    beyond = jnp.where((beyond < 0) | (beyond >= n_grp), grp ^ 1, beyond)
    at = jnp.stack([grp, (grp ^ beyond) // 2])

    def swap(value, axis, k):
        size = lax.axis_size(axis)
        return lax.ppermute(value, axis, [(i, i ^ k) for i in range(size)])

    def swap_next(value, axis):
        lower = range(1, lax.axis_size(axis) - 1, 2)
        return lax.ppermute(
            value, axis, [(i, i + 1) for i in lower] + [(i + 1, i) for i in lower]
        )

    def group_gather(value):
        parts = [value] + [swap(value, "grp", k) for k in range(2, n_grp, 2)]
        half = join_call(parts)
        return half, swap(half, "grp", 1)

    rounds = [
        lambda value: swap(value, "dev", 1),
        lambda value: swap_next(value, "dev"),
        lambda value: swap(value, "grp", 1),
        lambda value: swap_next(value, "grp"),
    ]

    def exchange(faces):
        return [turn(value) for turn, value in zip(rounds, faces)]

    local_map = coarse_map[0, 0]
    basis, onehot, *gradient = pack_call(
        odd, face_rows[0, 0], objective[0, 0], coarse_basis[0, 0], stiffness[0]
    )
    tile, *gradient = lax.optimization_barrier((coarse_inverse, *gradient))
    high, low = tile_call(tile.reshape(-1, tile.shape[3]))
    arrived = exchange(gradient)

    map_row = jnp.zeros((8, COLUMNS), jnp.float32)
    map_row = map_row.at[0, :LOCAL].set(local_map.astype(jnp.float32))
    high, low, map_row = lax.optimization_barrier((high, low, map_row))

    weighted, terms, weight, lift = weigh_call(gradient, arrived, basis, map_row, True)
    names = None
    adjoint = None
    lift_near = lift_far = None
    for sweep in range(SWEEPS):
        first = sweep == 0
        half, other = group_gather(terms)
        if first:
            names = other
        blocks = coarse_call(x_pos, half, other, high, low, n_grp, nz, nx)
        sent = [swap(blocks[k], "dev", k) for k in (2, 1, 3)]
        held, _ = lax.optimization_barrier((weighted, blocks[0]))
        near = local_call(onehot, held, local_inverse[0, 0], weight, lift, first)
        if SPLIT:
            far_grp = [rounds[p](near[p]) for p in (2, 3)]
            mine, *far_grp = lax.optimization_barrier((blocks[0], *far_grp))
        else:
            mine, *near = lax.optimization_barrier((blocks[0], *near))
        total = add_call(mine, *sent)
        total = lax.all_to_all(
            total.reshape(nz, OWNED, COLUMNS), "dev", 0, 0, axis_index_groups=z_groups, tiled=True
        )
        if SPLIT:
            far = [rounds[p](near[p]) for p in (0, 1)]
        else:
            far = exchange(near)
        total, *far = lax.optimization_barrier((total, *far))
        if SPLIT:
            far = far + far_grp
        owned = sum_call(total.reshape(nz * OWNED, COLUMNS))
        if first:
            lift_near, lift_far = near, far
        own, core, next_core = fetch_call(at, map_row, names, *group_gather(owned), n_grp)
        around = [rounds[0](own), rounds[1](own), core, next_core]
        if first:
            matrix, _ = lax.optimization_barrier((schur, own))
            ready = ready_call(near, far, gradient, matrix[0, 0])
            adjoint, *remain = middle_call(onehot, ready, around, own)
            weighted, terms = weigh_call(remain, exchange(remain), basis, map_row, False)
        else:
            kept, _ = lax.optimization_barrier((adjoint, own))
            ready = ready_last_call(near, far, lift_near, lift_far, kept)
            out = last_call(onehot, ready, around, own)
    return out[None, None]


def solution(mesh):
    return jax.shard_map(
        on_device,
        mesh=mesh,
        in_specs=(
            P("grp", "dev", None, None),
            P("grp", "dev", None, None),
            P("grp", "dev", None, None),
            P("grp", "dev", None, None),
            P(None, "dev", None, "grp"),
            P("grp", "dev", None),
            P("grp", "dev", None, None),
            P("grp", "dev", None),
        ),
        out_specs=P("grp", "dev", None, None),
        check_vma=False,
    )
```

```python
import functools

import jax
import jax.numpy as jnp
from jax import lax
from jax.experimental import pallas as pl
from jax.experimental.pallas import tpu as pltpu
from jax.sharding import PartitionSpec as P

INTERFACE = 1024
FACE_ROWS = 256
COLUMNS = 256
OWNED = 32
LOCAL = 64
SWEEPS = 2
X_SIZE = 4
TILE = 256
FACES = 4
TERM_ROWS = LOCAL + 8
MULT_ROWS = COLUMNS + 8

NN = (((1,), (0,)), ((), ()))
NT = (((1,), (1,)), ((), ()))
TN = (((0,), (0,)), ((), ()))

VMEM = pl.BlockSpec(memory_space=pltpu.VMEM)
SMEM = pl.BlockSpec(memory_space=pltpu.SMEM)
ANY = pl.BlockSpec(memory_space=pl.ANY)
HBM = "hbm"


def shaped(*shape, dtype=jnp.float32):
    return jax.ShapeDtypeStruct(shape, dtype)


def in_hbm(*shape, dtype=jnp.float32):
    return pltpu.HBM(shape, dtype)


def params():
    return pltpu.CompilerParams(vmem_limit_bytes=20 << 20)


def cost(flops, moved):
    return pl.CostEstimate(flops=flops, bytes_accessed=moved, transcendentals=0)


def call(kernel, name, out_shape, flops, moved, in_specs, scratch=()):
    outs = [VMEM if isinstance(o, jax.ShapeDtypeStruct) else ANY for o in out_shape]
    function = pl.pallas_call(
        kernel,
        out_shape=out_shape,
        in_specs=[ANY if spec is HBM else spec for spec in in_specs],
        out_specs=outs,
        scratch_shapes=scratch,
        compiler_params=params(),
        cost_estimate=cost(flops, moved),
        name=name,
    )

    def run(*values):
        values = [
            pltpu.with_memory_space_constraint(value, pltpu.HBM) if spec is HBM else value
            for value, spec in zip(values, in_specs)
        ]
        return function(*values)

    return run


def split(value):
    high = value.astype(jnp.bfloat16)
    low = (value - high.astype(jnp.float32)).astype(jnp.bfloat16)
    return high, low


def mul(left, right, dims):
    return lax.dot_general(left, right, dims, preferred_element_type=jnp.float32)


def mul3(left, right, dims):
    left_high, left_low = left
    right_high, right_low = right
    return (
        mul(left_high, right_low, dims)
        + mul(left_low, right_high, dims)
        + mul(left_high, right_high, dims)
    )


def folded(value):
    return value[:COLUMNS] + value[COLUMNS:]


def tile_at(t):
    return pl.ds(pl.multiple_of(t * TILE, TILE), TILE)


def face_at(p):
    return slice(p * FACE_ROWS, (p + 1) * FACE_ROWS)


def put(ref, at, value):
    ref[:COLUMNS, at], ref[COLUMNS:, at] = split(value)


PAIR = pltpu.VMEM((2 * COLUMNS, INTERFACE), jnp.bfloat16)
STEPS = INTERFACE // TILE
BASIS_AT = 2 * COLUMNS
MULT_AT = BASIS_AT + 2 * LOCAL


def fetched(source, target, sem):
    copy = pltpu.make_async_copy(source, target, sem)
    copy.start()
    return copy


def pack_kernel(
    odd_ref, slots_in, objective_in, basis_in, mult_in, basis_ref, onehot_ref, *rest
):
    outs = rest[:FACES]
    slots, staged, basis, mult, sems, left = rest[FACES:]
    slots_copy = fetched(slots_in, slots, sems.at[STEPS])
    small = [
        fetched(basis_in, basis, sems.at[STEPS + 1]),
        fetched(mult_in, mult, sems.at[STEPS + 2]),
    ]
    copies = [
        fetched(objective_in.at[t * TILE : (t + 1) * TILE], staged.at[t], sems.at[t])
        for t in range(STEPS)
    ]
    slots_copy.wait()
    odd_dev, odd_grp = odd_ref[0] == 1, odd_ref[1] == 1
    lines = [slots[p : p + 1] for p in range(FACES)]
    lines = [
        jnp.where(odd_dev, lines[0], lines[1]),
        jnp.where(odd_dev, lines[1], lines[0]),
        jnp.where(odd_grp, lines[2], lines[3]),
        jnp.where(odd_grp, lines[3], lines[2]),
    ]
    for p in range(FACES):
        rows = lax.broadcasted_iota(jnp.int32, (INTERFACE, FACE_ROWS), 0)
        onehot_ref[:, face_at(p)] = (
            (rows == lines[p]).astype(jnp.float32).astype(jnp.bfloat16)
        )
    for copy in small:
        copy.wait()
    left[BASIS_AT : BASIS_AT + LOCAL], left[BASIS_AT + LOCAL : MULT_AT] = split(basis[...])
    left[MULT_AT:] = jnp.broadcast_to(mult[...].astype(jnp.float32), (16, INTERFACE)).astype(
        jnp.bfloat16
    )
    for t in range(STEPS):
        copies[t].wait()
        at = slice(t * TILE, (t + 1) * TILE)
        left[:COLUMNS, at], left[COLUMNS:BASIS_AT, at] = split(staged[t].T)
    for p in range(FACES):
        out = mul(left[...], onehot_ref[:, face_at(p)], NN)
        outs[p][:COLUMNS] = folded(out[:BASIS_AT])
        outs[p][COLUMNS:] = out[MULT_AT : MULT_AT + 8]
        basis_ref[:, face_at(p)] = out[BASIS_AT : BASIS_AT + LOCAL] + out[BASIS_AT + LOCAL : MULT_AT]


def pack_call(odd, slots, objective, basis, mult):
    return call(
        pack_kernel,
        "pack",
        [shaped(LOCAL, INTERFACE), shaped(INTERFACE, INTERFACE, dtype=jnp.bfloat16)]
        + [shaped(MULT_ROWS, FACE_ROWS)] * FACES,
        2 << 30,
        4 << 20,
        [SMEM] + [HBM] * 4,
        scratch=[
            pltpu.VMEM((FACES, FACE_ROWS), jnp.int32),
            pltpu.VMEM((STEPS, TILE, COLUMNS), jnp.float32),
            pltpu.VMEM((LOCAL, INTERFACE), jnp.float32),
            pltpu.VMEM((1, INTERFACE), jnp.int32),
            pltpu.SemaphoreType.DMA((STEPS + 3,)),
            pltpu.VMEM((MULT_AT + 16, INTERFACE), jnp.bfloat16),
        ],
    )(odd, slots, objective, basis, mult)


def tile_kernel(tile_in, high_out, low_out, staged, sems, high, low, out_sems):
    copies = [
        fetched(tile_in.at[:, t * TILE : (t + 1) * TILE], staged.at[t], sems.at[t])
        for t in range(STEPS)
    ]
    outs = []
    for t in range(STEPS):
        copies[t].wait()
        at = slice(t * TILE, (t + 1) * TILE)
        high[at], low[at] = split(staged[t].T)
        outs.append(fetched(high.at[at], high_out.at[at], out_sems.at[0, t]))
        outs.append(fetched(low.at[at], low_out.at[at], out_sems.at[1, t]))
    for copy in outs:
        copy.wait()


def tile_call(tile):
    rows, width = tile.shape
    half = pltpu.VMEM((width, rows), jnp.bfloat16)
    return call(
        tile_kernel,
        "tile",
        [in_hbm(width, rows, dtype=jnp.bfloat16)] * 2,
        1 << 20,
        4 << 20,
        [HBM],
        scratch=[
            pltpu.VMEM((STEPS, rows, TILE), jnp.float32),
            pltpu.SemaphoreType.DMA((STEPS,)),
            half,
            half,
            pltpu.SemaphoreType.DMA((2, STEPS)),
        ],
    )(tile)


def join_kernel(*refs):
    rows = refs[0].shape[0]
    for i, ref in enumerate(refs[:-1]):
        refs[-1][i * rows : (i + 1) * rows] = ref[...]


def join_call(parts):
    rows, width = parts[0].shape
    (out,) = call(
        join_kernel,
        "join",
        [shaped(len(parts) * rows, width)],
        1 << 20,
        1 << 19,
        [VMEM] * len(parts),
    )(*parts)
    return out


def weigh_kernel(first, *refs):
    here, there = refs[:FACES], refs[FACES : 2 * FACES]
    basis_ref, map_ref = refs[2 * FACES : 2 * FACES + 2]
    weighted_out, terms_ref = refs[2 * FACES + 2 : 2 * FACES + 4]
    if first:
        weight_ref, lift_out, weighted_ref, sems, lift_ref = refs[2 * FACES + 4 :]
    else:
        weighted_ref, sems = refs[2 * FACES + 4 :]
    copies = []
    for p in range(FACES):
        mine = here[p][COLUMNS : COLUMNS + 1]
        total = mine + there[p][COLUMNS : COLUMNS + 1]
        weight = jnp.where(total > 0, mine / jnp.maximum(total, 1.0), 0.0)
        put(weighted_ref, face_at(p), weight * (here[p][:COLUMNS] + there[p][:COLUMNS]))
        at = (slice(None), face_at(p))
        copies.append(fetched(weighted_ref.at[at], weighted_out.at[at], sems.at[p]))
        if first:
            weight_ref[:, face_at(p)] = jnp.broadcast_to(weight, (8, FACE_ROWS))
            lift_ref[:, face_at(p)] = basis_ref[:, face_at(p)] * weight
            copies.append(fetched(lift_ref.at[at], lift_out.at[at], sems.at[FACES + p]))
    terms = jnp.zeros((LOCAL, COLUMNS), jnp.float32)
    for p in range(FACES):
        right = (weighted_ref[:COLUMNS, face_at(p)], weighted_ref[COLUMNS:, face_at(p)])
        terms = terms + mul3(split(basis_ref[:, face_at(p)]), right, NT)
    terms_ref[:LOCAL] = terms
    terms_ref[LOCAL:] = map_ref[...]
    for copy in copies:
        copy.wait()


def weigh_call(here, there, basis, map_row, first):
    out = [in_hbm(2 * COLUMNS, INTERFACE, dtype=jnp.bfloat16), shaped(TERM_ROWS, COLUMNS)]
    scratch = [PAIR, pltpu.SemaphoreType.DMA((2 * FACES,))]
    if first:
        out += [shaped(8, INTERFACE), in_hbm(LOCAL, INTERFACE)]
        scratch += [pltpu.VMEM((LOCAL, INTERFACE), jnp.float32)]
    return call(
        functools.partial(weigh_kernel, first),
        "weigh",
        out,
        100 << 20,
        2 << 20,
        [VMEM] * (2 * FACES + 2),
        scratch=scratch,
    )(*here, *there, basis, map_row)


def coarse_kernel(n_grp, nz, nx, x_ref, half_ref, other_ref, high_in, low_in, *rest):
    outs, (scratch, right, high_ref, low_ref, sems) = rest[: 2 * nx], rest[2 * nx :]

    def pieces(step):
        at = tile_at(step)
        return (
            pltpu.make_async_copy(high_in.at[at], high_ref.at[at], sems.at[0, step]),
            pltpu.make_async_copy(low_in.at[at], low_ref.at[at], sems.at[1, step]),
        )

    for step in range(STEPS):
        for copy in pieces(step):
            copy.start()
    dofs = n_grp * OWNED
    column = jnp.zeros((dofs, 2 * COLUMNS), jnp.float32)
    rows = lax.broadcasted_iota(jnp.int32, (dofs, LOCAL), 0).astype(jnp.float32)
    for ref in (half_ref, other_ref):
        for j in range(n_grp // 2):
            at = j * TERM_ROWS
            names = ref[at + LOCAL : at + LOCAL + 1, :LOCAL]
            onehot = (rows == names).astype(jnp.float32).astype(jnp.bfloat16)
            both = jnp.concatenate(split(ref[at : at + LOCAL, :]), axis=1)
            column = column + mul(onehot, both, NN)
    right[:, :COLUMNS], right[:, COLUMNS:] = split(column[:, :COLUMNS] + column[:, COLUMNS:])
    chunk = nx * OWNED
    per_step = TILE // chunk
    x_pos = x_ref[0]

    @pl.loop(0, nz // per_step)
    def _(step):
        at = tile_at(step)
        for copy in pieces(step):
            copy.wait()
        out = mul(high_ref[at, :], right[...], NN)
        scratch[...] = out[:, :COLUMNS] + (
            out[:, COLUMNS:] + mul(low_ref[at, :], right[:, :COLUMNS], NN)
        )
        for i in range(per_step):
            for k in range(nx):
                start = pl.multiple_of(i * chunk + (x_pos ^ k) * OWNED, OWNED)
                value = scratch[pl.ds(start, OWNED), :]
                z = step * per_step + i
                half = nz // 2

                @pl.when(z < half)
                def _():
                    outs[2 * k][pl.ds(pl.multiple_of(z * OWNED, OWNED), OWNED), :] = value

                @pl.when(z >= half)
                def _():
                    to = pl.multiple_of((z - half) * OWNED, OWNED)
                    outs[2 * k + 1][pl.ds(to, OWNED), :] = value


def coarse_call(x_pos, half, other, high, low, n_grp, nz, nx):
    return call(
        functools.partial(coarse_kernel, n_grp, nz, nx),
        "coarse",
        [shaped(nz // 2 * OWNED, COLUMNS)] * (2 * nx),
        600 << 20,
        3 << 20,
        [SMEM] + [VMEM] * 2 + [HBM] * 2,
        scratch=[
            pltpu.VMEM((TILE, COLUMNS), jnp.float32),
            pltpu.VMEM((n_grp * OWNED, 2 * COLUMNS), jnp.bfloat16),
            pltpu.VMEM(high.shape, high.dtype),
            pltpu.VMEM(low.shape, low.dtype),
            pltpu.SemaphoreType.DMA((2, STEPS)),
        ],
    )(x_pos, half, other, high, low)


def merge_kernel(left_ref, right_ref, out_ref):
    out_ref[...] = left_ref[...] + right_ref[...]


def merge_call(left, right):
    (out,) = call(
        merge_kernel, "merge", [shaped(*left.shape)], 1 << 18, 1 << 18, [VMEM] * 2
    )(left, right)
    return out


def add_kernel(*refs):
    out_ref, staged, sems = refs[6:]
    rows = refs[0].shape[0]
    copies = []
    for i in range(2):
        at = slice(i * rows, (i + 1) * rows)
        staged[at] = refs[3 * i][...] + refs[3 * i + 1][...] + refs[3 * i + 2][...]
        copies.append(fetched(staged.at[at], out_ref.at[at], sems.at[i]))
    for copy in copies:
        copy.wait()


def add_call(*values):
    rows, width = values[0].shape
    (out,) = call(
        add_kernel,
        "add",
        [in_hbm(2 * rows, width)],
        1 << 20,
        1 << 20,
        [VMEM] * len(values),
        scratch=[pltpu.VMEM((2 * rows, width), jnp.float32), pltpu.SemaphoreType.DMA((2,))],
    )(*values)
    return out


def sum_kernel(count, value_ref, out_ref):
    value = value_ref[:OWNED]
    for i in range(1, count):
        value = value + value_ref[i * OWNED : (i + 1) * OWNED]
    out_ref[...] = value


def sum_call(value):
    (out,) = call(
        functools.partial(sum_kernel, value.shape[0] // OWNED),
        "sum",
        [shaped(OWNED, COLUMNS)],
        1 << 20,
        1 << 18,
        [VMEM],
    )(value)
    return out


def update_kernel(n_grp, at_ref, map_ref, half_ref, other_ref, lift_in, *rest):
    near_in, outs = rest[:FACES], rest[FACES : 2 * FACES]
    lift, near, sems = rest[2 * FACES :]
    lift_copy = fetched(lift_in, lift, sems.at[FACES])
    copies = [fetched(near_in[p], near.at[p], sems.at[p]) for p in range(FACES)]
    dofs = n_grp * OWNED
    index = lax.broadcasted_iota(jnp.int32, (dofs, LOCAL), 0)
    block, inside = index // OWNED, index % OWNED
    block = jnp.where(block < n_grp // 2, 2 * block, 2 * block - n_grp + 1)
    ids = ((block ^ at_ref[0]) * OWNED + inside).astype(jnp.float32)
    value = jnp.concatenate([half_ref[...], other_ref[...]], axis=0)
    both = jnp.concatenate(split(value), axis=1)
    onehot = (ids == map_ref[:1, :LOCAL]).astype(jnp.float32).astype(jnp.bfloat16)
    pair = mul(onehot, both, TN)
    own = split(pair[:, :COLUMNS] + pair[:, COLUMNS:])
    lift_copy.wait()
    for p in range(FACES):
        copies[p].wait()
        outs[p][...] = near[p] + mul3(own, split(lift[:, face_at(p)]), TN)


def update_call(at, map_row, half, other, lift, near, n_grp):
    return call(
        functools.partial(update_kernel, n_grp),
        "update",
        [shaped(COLUMNS, FACE_ROWS)] * FACES,
        300 << 20,
        3 << 20,
        [SMEM] + [VMEM] * 3 + [HBM] * (1 + FACES),
        scratch=[
            pltpu.VMEM((LOCAL, INTERFACE), jnp.float32),
            pltpu.VMEM((FACES, COLUMNS, FACE_ROWS), jnp.float32),
            pltpu.SemaphoreType.DMA((FACES + 1,)),
        ],
    )(at, map_row, half, other, lift, *near)


def matrix_copy(matrix_in, matrix, sems, t):
    at = tile_at(t)
    return pltpu.make_async_copy(matrix_in.at[:, at], matrix.at[:, at], sems.at[t])


def start_matrix(matrix_in, matrix, sems, tiles):
    for t in tiles:
        matrix_copy(matrix_in, matrix, sems, t).start()


def to_rows(onehot_ref, value_ref, rows_ref):
    @pl.loop(0, STEPS)
    def _(t):
        put(rows_ref, tile_at(t), folded(mul(value_ref[...], onehot_ref[tile_at(t), :], NT)))


def product(rows_ref, high, low):
    return folded(mul(rows_ref[...], high, NN)) + mul(rows_ref[:COLUMNS], low, NN)


MATRIX = [
    pltpu.VMEM((INTERFACE, INTERFACE), jnp.float32),
    pltpu.SemaphoreType.DMA((STEPS,)),
]


def local_kernel(onehot_ref, weighted_in, matrix_in, weight_ref, *rest):
    outs = rest[:FACES]
    matrix, matrix_sems, weighted, sems, rows, result, staged = rest[FACES:]
    weighted_copy = fetched(weighted_in, weighted, sems.at[0])
    start_matrix(matrix_in, matrix, matrix_sems, range(2))
    weighted_copy.wait()
    start_matrix(matrix_in, matrix, matrix_sems, range(2, STEPS))
    to_rows(onehot_ref, weighted, rows)

    @pl.loop(0, STEPS)
    def _(t):
        matrix_copy(matrix_in, matrix, matrix_sems, t).wait()
        put(result, tile_at(t), product(rows, *split(matrix[:, tile_at(t)])))

    copies = []
    for p in range(FACES):
        out = folded(mul(result[...], onehot_ref[:, face_at(p)], NN))
        staged[p] = weight_ref[:1, face_at(p)] * out
        copies.append(fetched(staged.at[p], outs[p], sems.at[1 + p]))
    for copy in copies:
        copy.wait()


def local_call(onehot, weighted, matrix, weight):
    return call(
        local_kernel,
        "local",
        [in_hbm(COLUMNS, FACE_ROWS)] * FACES,
        6 << 30,
        8 << 20,
        [VMEM, HBM, HBM, VMEM],
        scratch=MATRIX
        + [PAIR, pltpu.SemaphoreType.DMA((1 + FACES,))]
        + [PAIR] * 2
        + [pltpu.VMEM((FACES, COLUMNS, FACE_ROWS), jnp.float32)],
    )(onehot, weighted, matrix, weight)


BODY = slice(0, COLUMNS)
FACE_BLOCK = pltpu.VMEM((FACES, COLUMNS, FACE_ROWS), jnp.float32)


def ready_kernel(*refs):
    gradient_in, matrix_in = refs[:FACES], refs[FACES]
    gradient_ref, high_ref, low_ref, matrix, matrix_sems, sems = refs[FACES + 1 :]
    start_matrix(matrix_in, matrix, matrix_sems, range(STEPS))
    copies = [fetched(gradient_in[p], gradient_ref.at[p], sems.at[p]) for p in range(FACES)]

    @pl.loop(0, STEPS)
    def _(t):
        matrix_copy(matrix_in, matrix, matrix_sems, t).wait()
        high_ref[:, tile_at(t)], low_ref[:, tile_at(t)] = split(matrix[:, tile_at(t)])

    for copy in copies:
        copy.wait()


def ready_call(gradient, matrix):
    half = shaped(INTERFACE, INTERFACE, dtype=jnp.bfloat16)
    return call(
        ready_kernel,
        "ready",
        [shaped(FACES, MULT_ROWS, FACE_ROWS), half, half],
        4 << 20,
        8 << 20,
        [HBM] * (FACES + 1),
        scratch=MATRIX + [pltpu.SemaphoreType.DMA((FACES,))],
    )(*gradient, matrix)


def ready_last_kernel(adjoint_in, adjoint_ref, sem):
    fetched(adjoint_in, adjoint_ref, sem).wait()


def ready_last_call(adjoint):
    (out,) = call(
        ready_last_kernel,
        "ready_last",
        [shaped(FACES, COLUMNS, FACE_ROWS)],
        1 << 20,
        2 << 20,
        [HBM],
        scratch=[pltpu.SemaphoreType.DMA],
    )(adjoint)
    return out


def middle_kernel(onehot_ref, gradient_ref, high_ref, low_ref, *refs):
    near, far, adjoint_out = refs[:FACES], refs[FACES : 2 * FACES], refs[2 * FACES]
    outs = refs[2 * FACES + 1 : 3 * FACES + 1]
    sems, kept, value, rows, result = refs[3 * FACES + 1 :]
    copies = []
    for p in range(FACES):
        adjoint = near[p][...] + far[p][...]
        kept[p] = adjoint
        copies.append(fetched(kept.at[p], adjoint_out.at[p], sems.at[p]))
        put(value, face_at(p), adjoint)
    to_rows(onehot_ref, value, rows)

    @pl.loop(0, STEPS)
    def _(t):
        put(result, tile_at(t), product(rows, high_ref[:, tile_at(t)], low_ref[:, tile_at(t)]))

    for p in range(FACES):
        out = folded(mul(result[...], onehot_ref[:, face_at(p)], NN))
        outs[p][:COLUMNS] = gradient_ref[p, BODY] - out
        outs[p][COLUMNS:] = gradient_ref[p, COLUMNS:]
    for copy in copies:
        copy.wait()


def middle_call(onehot, ready, near, far):
    return call(
        middle_kernel,
        "middle",
        [in_hbm(FACES, COLUMNS, FACE_ROWS)] + [shaped(MULT_ROWS, FACE_ROWS)] * FACES,
        6 << 30,
        12 << 20,
        [VMEM] * (4 + 2 * FACES),
        scratch=[pltpu.SemaphoreType.DMA((FACES,)), FACE_BLOCK] + [PAIR] * 3,
    )(onehot, *ready, *near, *far)


def last_kernel(onehot_ref, adjoint_ref, *refs):
    near, far = refs[:FACES], refs[FACES : 2 * FACES]
    out_ref, value, staged, sems = refs[2 * FACES :]
    for p in range(FACES):
        put(value, face_at(p), adjoint_ref[p] + near[p][...] + far[p][...])
    copies = []
    for t in range(STEPS):
        at = slice(t * TILE, (t + 1) * TILE)
        out = mul(onehot_ref[at, :], value[...], NT)
        staged[t] = out[:, :COLUMNS] + out[:, COLUMNS:]
        copies.append(fetched(staged.at[t], out_ref.at[at], sems.at[t]))
    for copy in copies:
        copy.wait()


def last_call(onehot, adjoint, near, far):
    (out,) = call(
        last_kernel,
        "last",
        [in_hbm(INTERFACE, COLUMNS)],
        1 << 30,
        6 << 20,
        [VMEM] * (2 + 2 * FACES),
        scratch=[
            PAIR,
            pltpu.VMEM((STEPS, TILE, COLUMNS), jnp.float32),
            pltpu.SemaphoreType.DMA((STEPS,)),
        ],
    )(onehot, adjoint, *near, *far)
    return out


def on_device(
    objective, schur, local_inverse, coarse_basis, coarse_inverse, stiffness, face_rows, coarse_map
):
    n_grp, n_dev = lax.axis_size("grp"), lax.axis_size("dev")
    nx = X_SIZE
    nz = n_dev // nx
    grp = lax.axis_index("grp").astype(jnp.int32)
    dev = lax.axis_index("dev").astype(jnp.int32)
    x_pos = (dev % nx).reshape(1)
    z_groups = [[z * nx + x for z in range(nz)] for x in range(nx)]
    odd = jnp.stack([dev % 2, grp % 2])
    at = grp.reshape(1)

    def swap(value, axis, k):
        size = lax.axis_size(axis)
        return lax.ppermute(value, axis, [(i, i ^ k) for i in range(size)])

    def swap_next(value, axis):
        lower = range(1, lax.axis_size(axis) - 1, 2)
        return lax.ppermute(
            value, axis, [(i, i + 1) for i in lower] + [(i + 1, i) for i in lower]
        )

    def group_gather(value):
        parts = {k: swap(value, "grp", k) for k in (2, 6, 4)}
        parts = [value] + [parts[k] for k in range(2, n_grp, 2)]
        half = join_call(parts)
        return half, swap(half, "grp", 1)

    rounds = [
        lambda value: swap(value, "dev", 1),
        lambda value: swap_next(value, "dev"),
        lambda value: swap(value, "grp", 1),
        lambda value: swap_next(value, "grp"),
    ]

    def exchange(faces):
        return [turn(value) for turn, value in zip(rounds, faces)]

    local_map = coarse_map[0, 0]
    basis, onehot, *gradient = pack_call(
        odd, face_rows[0, 0], objective[0, 0], coarse_basis[0, 0], stiffness[0]
    )
    tile, *gradient = lax.optimization_barrier((coarse_inverse, *gradient))
    high, low = tile_call(tile.reshape(-1, tile.shape[3]))
    arrived = exchange(gradient)

    map_row = jnp.zeros((8, COLUMNS), jnp.float32)
    map_row = map_row.at[0, :LOCAL].set(local_map.astype(jnp.float32))
    high, low, map_row = lax.optimization_barrier((high, low, map_row))

    weighted, terms, weight, lift = weigh_call(gradient, arrived, basis, map_row, True)
    adjoint = None
    for sweep in range(SWEEPS):
        first = sweep == 0
        half, other = group_gather(terms)
        blocks = coarse_call(x_pos, half, other, high, low, n_grp, nz, nx)
        through = [swap(blocks[4], "dev", 1), swap(blocks[5], "dev", 3)]
        direct = [swap(blocks[2], "dev", 1), swap(blocks[7], "dev", 3)]
        passed = [
            swap(merge_call(blocks[6], through[0]), "dev", 3),
            swap(merge_call(blocks[3], through[1]), "dev", 1),
        ]
        total = add_call(blocks[0], direct[0], passed[0], blocks[1], passed[1], direct[1])
        total = lax.all_to_all(
            total.reshape(nz, OWNED, COLUMNS), "dev", 0, 0, axis_index_groups=z_groups, tiled=True
        )
        held, _ = lax.optimization_barrier((weighted, direct[0]))
        near = local_call(onehot, held, local_inverse[0, 0], weight)
        total, *near = lax.optimization_barrier((total, *near))
        owned = sum_call(total.reshape(nz * OWNED, COLUMNS))
        half, other = group_gather(owned)
        near = update_call(at, map_row, half, other, lift, near, n_grp)
        far = exchange(near)
        if first:
            matrix, _ = lax.optimization_barrier((schur, near[0]))
            ready = ready_call(gradient, matrix[0, 0])
            adjoint, *remain = middle_call(onehot, ready, near, far)
            weighted, terms = weigh_call(remain, exchange(remain), basis, map_row, False)
        else:
            kept, _ = lax.optimization_barrier((adjoint, near[0]))
            out = last_call(onehot, ready_last_call(kept), near, far)
    return out[None, None]


def solution(mesh):
    return jax.shard_map(
        on_device,
        mesh=mesh,
        in_specs=(
            P("grp", "dev", None, None),
            P("grp", "dev", None, None),
            P("grp", "dev", None, None),
            P("grp", "dev", None, None),
            P(None, "dev", None, "grp"),
            P("grp", "dev", None),
            P("grp", "dev", None, None),
            P("grp", "dev", None),
        ),
        out_specs=P("grp", "dev", None, None),
        check_vma=False,
    )
```

```python
import functools

import jax
import jax.numpy as jnp
from jax import lax
from jax.experimental import pallas as pl
from jax.experimental.pallas import tpu as pltpu
from jax.sharding import PartitionSpec as P

INTERFACE = 1024
FACE_ROWS = 256
COLUMNS = 256
OWNED = 32
LOCAL = 64
SWEEPS = 2
X_SIZE = 4
TILE = 256
FACES = 4
TERM_ROWS = LOCAL + 8
MULT_ROWS = COLUMNS + 8

NN = (((1,), (0,)), ((), ()))
NT = (((1,), (1,)), ((), ()))
TN = (((0,), (0,)), ((), ()))

VMEM = pl.BlockSpec(memory_space=pltpu.VMEM)
SMEM = pl.BlockSpec(memory_space=pltpu.SMEM)
ANY = pl.BlockSpec(memory_space=pl.ANY)
HBM = "hbm"


def shaped(*shape, dtype=jnp.float32):
    return jax.ShapeDtypeStruct(shape, dtype)


def in_hbm(*shape, dtype=jnp.float32):
    return pltpu.HBM(shape, dtype)


def params():
    return pltpu.CompilerParams(vmem_limit_bytes=20 << 20)


def cost(flops, moved):
    return pl.CostEstimate(flops=flops, bytes_accessed=moved, transcendentals=0)


def call(kernel, name, out_shape, flops, moved, in_specs, scratch=()):
    outs = [VMEM if isinstance(o, jax.ShapeDtypeStruct) else ANY for o in out_shape]
    function = pl.pallas_call(
        kernel,
        out_shape=out_shape,
        in_specs=[ANY if spec is HBM else spec for spec in in_specs],
        out_specs=outs,
        scratch_shapes=scratch,
        compiler_params=params(),
        cost_estimate=cost(flops, moved),
        name=name,
    )

    def run(*values):
        values = [
            pltpu.with_memory_space_constraint(value, pltpu.HBM) if spec is HBM else value
            for value, spec in zip(values, in_specs)
        ]
        return function(*values)

    return run


def split(value):
    high = value.astype(jnp.bfloat16)
    low = (value - high.astype(jnp.float32)).astype(jnp.bfloat16)
    return high, low


def mul(left, right, dims):
    return lax.dot_general(left, right, dims, preferred_element_type=jnp.float32)


def mul3(left, right, dims):
    left_high, left_low = left
    right_high, right_low = right
    return (
        mul(left_high, right_low, dims)
        + mul(left_low, right_high, dims)
        + mul(left_high, right_high, dims)
    )


def folded(value):
    return value[:COLUMNS] + value[COLUMNS:]


def tile_at(t):
    return pl.ds(pl.multiple_of(t * TILE, TILE), TILE)


def face_at(p):
    return slice(p * FACE_ROWS, (p + 1) * FACE_ROWS)


def put(ref, at, value):
    ref[:COLUMNS, at], ref[COLUMNS:, at] = split(value)


PAIR = pltpu.VMEM((2 * COLUMNS, INTERFACE), jnp.bfloat16)
STEPS = INTERFACE // TILE
BASIS_AT = 2 * COLUMNS
MULT_AT = BASIS_AT + 2 * LOCAL


def fetched(source, target, sem):
    copy = pltpu.make_async_copy(source, target, sem)
    copy.start()
    return copy


def pack_kernel(
    odd_ref, slots_in, objective_in, basis_in, mult_in, basis_ref, onehot_ref, *rest
):
    outs = rest[:FACES]
    slots, staged, basis, mult, sems, left = rest[FACES:]
    slots_copy = fetched(slots_in, slots, sems.at[STEPS])
    small = [
        fetched(basis_in, basis, sems.at[STEPS + 1]),
        fetched(mult_in, mult, sems.at[STEPS + 2]),
    ]
    copies = [
        fetched(objective_in.at[t * TILE : (t + 1) * TILE], staged.at[t], sems.at[t])
        for t in range(STEPS)
    ]
    slots_copy.wait()
    odd_dev, odd_grp = odd_ref[0] == 1, odd_ref[1] == 1
    lines = [slots[p : p + 1] for p in range(FACES)]
    lines = [
        jnp.where(odd_dev, lines[0], lines[1]),
        jnp.where(odd_dev, lines[1], lines[0]),
        jnp.where(odd_grp, lines[2], lines[3]),
        jnp.where(odd_grp, lines[3], lines[2]),
    ]
    for p in range(FACES):
        rows = lax.broadcasted_iota(jnp.int32, (INTERFACE, FACE_ROWS), 0)
        onehot_ref[:, face_at(p)] = (
            (rows == lines[p]).astype(jnp.float32).astype(jnp.bfloat16)
        )
    for copy in small:
        copy.wait()
    left[BASIS_AT : BASIS_AT + LOCAL], left[BASIS_AT + LOCAL : MULT_AT] = split(basis[...])
    left[MULT_AT:] = jnp.broadcast_to(mult[...].astype(jnp.float32), (16, INTERFACE)).astype(
        jnp.bfloat16
    )
    for t in range(STEPS):
        copies[t].wait()
        at = slice(t * TILE, (t + 1) * TILE)
        left[:COLUMNS, at], left[COLUMNS:BASIS_AT, at] = split(staged[t].T)
    for p in range(FACES):
        out = mul(left[...], onehot_ref[:, face_at(p)], NN)
        outs[p][:COLUMNS] = folded(out[:BASIS_AT])
        outs[p][COLUMNS:] = out[MULT_AT : MULT_AT + 8]
        basis_ref[:, face_at(p)] = out[BASIS_AT : BASIS_AT + LOCAL] + out[BASIS_AT + LOCAL : MULT_AT]


def pack_call(odd, slots, objective, basis, mult):
    return call(
        pack_kernel,
        "pack",
        [shaped(LOCAL, INTERFACE), shaped(INTERFACE, INTERFACE, dtype=jnp.bfloat16)]
        + [shaped(MULT_ROWS, FACE_ROWS)] * FACES,
        2 << 30,
        4 << 20,
        [SMEM] + [HBM] * 4,
        scratch=[
            pltpu.VMEM((FACES, FACE_ROWS), jnp.int32),
            pltpu.VMEM((STEPS, TILE, COLUMNS), jnp.float32),
            pltpu.VMEM((LOCAL, INTERFACE), jnp.float32),
            pltpu.VMEM((1, INTERFACE), jnp.int32),
            pltpu.SemaphoreType.DMA((STEPS + 3,)),
            pltpu.VMEM((MULT_AT + 16, INTERFACE), jnp.bfloat16),
        ],
    )(odd, slots, objective, basis, mult)


def tile_kernel(tile_in, high_out, low_out, staged, sems, high, low, out_sems):
    copies = [
        fetched(tile_in.at[:, t * TILE : (t + 1) * TILE], staged.at[t], sems.at[t])
        for t in range(STEPS)
    ]
    outs = []
    for t in range(STEPS):
        copies[t].wait()
        at = slice(t * TILE, (t + 1) * TILE)
        high[at], low[at] = split(staged[t].T)
        outs.append(fetched(high.at[at], high_out.at[at], out_sems.at[0, t]))
        outs.append(fetched(low.at[at], low_out.at[at], out_sems.at[1, t]))
    for copy in outs:
        copy.wait()


def tile_call(tile):
    rows, width = tile.shape
    half = pltpu.VMEM((width, rows), jnp.bfloat16)
    return call(
        tile_kernel,
        "tile",
        [in_hbm(width, rows, dtype=jnp.bfloat16)] * 2,
        1 << 20,
        4 << 20,
        [HBM],
        scratch=[
            pltpu.VMEM((STEPS, rows, TILE), jnp.float32),
            pltpu.SemaphoreType.DMA((STEPS,)),
            half,
            half,
            pltpu.SemaphoreType.DMA((2, STEPS)),
        ],
    )(tile)


def join_kernel(*refs):
    rows = refs[0].shape[0]
    for i, ref in enumerate(refs[:-1]):
        refs[-1][i * rows : (i + 1) * rows] = ref[...]


def join_call(parts):
    rows, width = parts[0].shape
    (out,) = call(
        join_kernel,
        "join",
        [shaped(len(parts) * rows, width)],
        1 << 20,
        1 << 19,
        [VMEM] * len(parts),
    )(*parts)
    return out


def weigh_kernel(first, *refs):
    here, there = refs[:FACES], refs[FACES : 2 * FACES]
    basis_ref, map_ref = refs[2 * FACES : 2 * FACES + 2]
    weighted_out, terms_ref = refs[2 * FACES + 2 : 2 * FACES + 4]
    if first:
        weight_ref, lift_out, weighted_ref, sems, lift_ref = refs[2 * FACES + 4 :]
    else:
        weighted_ref, sems = refs[2 * FACES + 4 :]
    copies = []
    for p in range(FACES):
        mine = here[p][COLUMNS : COLUMNS + 1]
        total = mine + there[p][COLUMNS : COLUMNS + 1]
        weight = jnp.where(total > 0, mine / jnp.maximum(total, 1.0), 0.0)
        put(weighted_ref, face_at(p), weight * (here[p][:COLUMNS] + there[p][:COLUMNS]))
        at = (slice(None), face_at(p))
        copies.append(fetched(weighted_ref.at[at], weighted_out.at[at], sems.at[p]))
        if first:
            weight_ref[:, face_at(p)] = jnp.broadcast_to(weight, (8, FACE_ROWS))
            lift_ref[:, face_at(p)] = basis_ref[:, face_at(p)] * weight
            copies.append(fetched(lift_ref.at[at], lift_out.at[at], sems.at[FACES + p]))
    terms = jnp.zeros((LOCAL, COLUMNS), jnp.float32)
    for p in range(FACES):
        right = (weighted_ref[:COLUMNS, face_at(p)], weighted_ref[COLUMNS:, face_at(p)])
        terms = terms + mul3(split(basis_ref[:, face_at(p)]), right, NT)
    terms_ref[:LOCAL] = terms
    terms_ref[LOCAL:] = map_ref[...]
    for copy in copies:
        copy.wait()


def weigh_call(here, there, basis, map_row, first):
    out = [in_hbm(2 * COLUMNS, INTERFACE, dtype=jnp.bfloat16), shaped(TERM_ROWS, COLUMNS)]
    scratch = [PAIR, pltpu.SemaphoreType.DMA((2 * FACES,))]
    if first:
        out += [shaped(8, INTERFACE), in_hbm(LOCAL, INTERFACE)]
        scratch += [pltpu.VMEM((LOCAL, INTERFACE), jnp.float32)]
    return call(
        functools.partial(weigh_kernel, first),
        "weigh",
        out,
        100 << 20,
        2 << 20,
        [VMEM] * (2 * FACES + 2),
        scratch=scratch,
    )(*here, *there, basis, map_row)


def coarse_kernel(n_grp, nz, nx, x_ref, half_ref, other_ref, high_in, low_in, *rest):
    outs, (scratch, right, high_ref, low_ref, sems) = rest[: 2 * nx], rest[2 * nx :]

    def pieces(step):
        at = tile_at(step)
        return (
            pltpu.make_async_copy(high_in.at[at], high_ref.at[at], sems.at[0, step]),
            pltpu.make_async_copy(low_in.at[at], low_ref.at[at], sems.at[1, step]),
        )

    for step in range(STEPS):
        for copy in pieces(step):
            copy.start()
    dofs = n_grp * OWNED
    column = jnp.zeros((dofs, 2 * COLUMNS), jnp.float32)
    rows = lax.broadcasted_iota(jnp.int32, (dofs, LOCAL), 0).astype(jnp.float32)
    for ref in (half_ref, other_ref):
        for j in range(n_grp // 2):
            at = j * TERM_ROWS
            names = ref[at + LOCAL : at + LOCAL + 1, :LOCAL]
            onehot = (rows == names).astype(jnp.float32).astype(jnp.bfloat16)
            both = jnp.concatenate(split(ref[at : at + LOCAL, :]), axis=1)
            column = column + mul(onehot, both, NN)
    right[:, :COLUMNS], right[:, COLUMNS:] = split(column[:, :COLUMNS] + column[:, COLUMNS:])
    chunk = nx * OWNED
    per_step = TILE // chunk
    x_pos = x_ref[0]

    @pl.loop(0, nz // per_step)
    def _(step):
        at = tile_at(step)
        for copy in pieces(step):
            copy.wait()
        out = mul(high_ref[at, :], right[...], NN)
        scratch[...] = out[:, :COLUMNS] + (
            out[:, COLUMNS:] + mul(low_ref[at, :], right[:, :COLUMNS], NN)
        )
        for i in range(per_step):
            for k in range(nx):
                start = pl.multiple_of(i * chunk + (x_pos ^ k) * OWNED, OWNED)
                value = scratch[pl.ds(start, OWNED), :]
                z = step * per_step + i
                half = nz // 2

                @pl.when(z < half)
                def _():
                    outs[2 * k][pl.ds(pl.multiple_of(z * OWNED, OWNED), OWNED), :] = value

                @pl.when(z >= half)
                def _():
                    to = pl.multiple_of((z - half) * OWNED, OWNED)
                    outs[2 * k + 1][pl.ds(to, OWNED), :] = value


def coarse_call(x_pos, half, other, high, low, n_grp, nz, nx):
    return call(
        functools.partial(coarse_kernel, n_grp, nz, nx),
        "coarse",
        [shaped(nz // 2 * OWNED, COLUMNS)] * (2 * nx),
        600 << 20,
        3 << 20,
        [SMEM] + [VMEM] * 2 + [HBM] * 2,
        scratch=[
            pltpu.VMEM((TILE, COLUMNS), jnp.float32),
            pltpu.VMEM((n_grp * OWNED, 2 * COLUMNS), jnp.bfloat16),
            pltpu.VMEM(high.shape, high.dtype),
            pltpu.VMEM(low.shape, low.dtype),
            pltpu.SemaphoreType.DMA((2, STEPS)),
        ],
    )(x_pos, half, other, high, low)


def merge_kernel(left_ref, right_ref, out_ref):
    out_ref[...] = left_ref[...] + right_ref[...]


def merge_call(left, right):
    (out,) = call(
        merge_kernel, "merge", [shaped(*left.shape)], 1 << 18, 1 << 18, [VMEM] * 2
    )(left, right)
    return out


def add_kernel(*refs):
    out_ref, staged, sems = refs[6:]
    rows = refs[0].shape[0]
    copies = []
    for i in range(2):
        at = slice(i * rows, (i + 1) * rows)
        staged[at] = refs[3 * i][...] + refs[3 * i + 1][...] + refs[3 * i + 2][...]
        copies.append(fetched(staged.at[at], out_ref.at[at], sems.at[i]))
    for copy in copies:
        copy.wait()


def add_call(*values):
    rows, width = values[0].shape
    (out,) = call(
        add_kernel,
        "add",
        [in_hbm(2 * rows, width)],
        1 << 20,
        1 << 20,
        [VMEM] * len(values),
        scratch=[pltpu.VMEM((2 * rows, width), jnp.float32), pltpu.SemaphoreType.DMA((2,))],
    )(*values)
    return out


def sum_kernel(count, value_ref, out_ref):
    value = value_ref[:OWNED]
    for i in range(1, count):
        value = value + value_ref[i * OWNED : (i + 1) * OWNED]
    out_ref[...] = value


def sum_call(value):
    (out,) = call(
        functools.partial(sum_kernel, value.shape[0] // OWNED),
        "sum",
        [shaped(OWNED, COLUMNS)],
        1 << 20,
        1 << 18,
        [VMEM],
    )(value)
    return out


def bring_kernel(lift_in, *refs):
    near_in, (lift_ref, near_ref, sems) = refs[:FACES], refs[FACES:]
    copies = [fetched(lift_in, lift_ref, sems.at[FACES])]
    copies += [fetched(near_in[p], near_ref.at[p], sems.at[p]) for p in range(FACES)]
    for copy in copies:
        copy.wait()


def bring_call(lift, near):
    return call(
        bring_kernel,
        "bring",
        [shaped(LOCAL, INTERFACE), shaped(FACES, COLUMNS, FACE_ROWS)],
        1 << 20,
        2 << 20,
        [HBM] * (1 + FACES),
        scratch=[pltpu.SemaphoreType.DMA((FACES + 1,))],
    )(lift, *near)


def update_kernel(n_grp, at_ref, map_ref, half_ref, other_ref, lift, near, *outs):
    dofs = n_grp * OWNED
    index = lax.broadcasted_iota(jnp.int32, (dofs, LOCAL), 0)
    block, inside = index // OWNED, index % OWNED
    block = jnp.where(block < n_grp // 2, 2 * block, 2 * block - n_grp + 1)
    ids = ((block ^ at_ref[0]) * OWNED + inside).astype(jnp.float32)
    value = jnp.concatenate([half_ref[...], other_ref[...]], axis=0)
    both = jnp.concatenate(split(value), axis=1)
    onehot = (ids == map_ref[:1, :LOCAL]).astype(jnp.float32).astype(jnp.bfloat16)
    pair = mul(onehot, both, TN)
    own = split(pair[:, :COLUMNS] + pair[:, COLUMNS:])
    for p in range(FACES):
        outs[p][...] = near[p] + mul3(own, split(lift[:, face_at(p)]), TN)


def update_call(at, map_row, half, other, lift, near, n_grp):
    return call(
        functools.partial(update_kernel, n_grp),
        "update",
        [shaped(COLUMNS, FACE_ROWS)] * FACES,
        300 << 20,
        3 << 20,
        [SMEM] + [VMEM] * 5,
    )(at, map_row, half, other, lift, near)


def matrix_copy(matrix_in, matrix, sems, t):
    at = tile_at(t)
    return pltpu.make_async_copy(matrix_in.at[:, at], matrix.at[:, at], sems.at[t])


def start_matrix(matrix_in, matrix, sems, tiles):
    for t in tiles:
        matrix_copy(matrix_in, matrix, sems, t).start()


def to_rows(onehot_ref, value_ref, rows_ref):
    @pl.loop(0, STEPS)
    def _(t):
        put(rows_ref, tile_at(t), folded(mul(value_ref[...], onehot_ref[tile_at(t), :], NT)))


def product(rows_ref, high, low):
    return folded(mul(rows_ref[...], high, NN)) + mul(rows_ref[:COLUMNS], low, NN)


MATRIX = [
    pltpu.VMEM((INTERFACE, INTERFACE), jnp.float32),
    pltpu.SemaphoreType.DMA((STEPS,)),
]


def local_kernel(onehot_ref, weighted_in, matrix_in, weight_ref, *rest):
    outs = rest[:FACES]
    matrix, matrix_sems, weighted, sems, rows, result, staged = rest[FACES:]
    weighted_copy = fetched(weighted_in, weighted, sems.at[0])
    start_matrix(matrix_in, matrix, matrix_sems, range(2))
    weighted_copy.wait()
    start_matrix(matrix_in, matrix, matrix_sems, range(2, STEPS))
    to_rows(onehot_ref, weighted, rows)

    @pl.loop(0, STEPS)
    def _(t):
        matrix_copy(matrix_in, matrix, matrix_sems, t).wait()
        put(result, tile_at(t), product(rows, *split(matrix[:, tile_at(t)])))

    copies = []
    for p in range(FACES):
        out = folded(mul(result[...], onehot_ref[:, face_at(p)], NN))
        staged[p] = weight_ref[:1, face_at(p)] * out
        copies.append(fetched(staged.at[p], outs[p], sems.at[1 + p]))
    for copy in copies:
        copy.wait()


def local_call(onehot, weighted, matrix, weight):
    return call(
        local_kernel,
        "local",
        [in_hbm(COLUMNS, FACE_ROWS)] * FACES,
        6 << 30,
        8 << 20,
        [VMEM, HBM, HBM, VMEM],
        scratch=MATRIX
        + [PAIR, pltpu.SemaphoreType.DMA((1 + FACES,))]
        + [PAIR] * 2
        + [pltpu.VMEM((FACES, COLUMNS, FACE_ROWS), jnp.float32)],
    )(onehot, weighted, matrix, weight)


BODY = slice(0, COLUMNS)
FACE_BLOCK = pltpu.VMEM((FACES, COLUMNS, FACE_ROWS), jnp.float32)


def ready_kernel(*refs):
    gradient_in, matrix_in = refs[:FACES], refs[FACES]
    gradient_ref, high_ref, low_ref, matrix, matrix_sems, sems = refs[FACES + 1 :]
    start_matrix(matrix_in, matrix, matrix_sems, range(STEPS))
    copies = [fetched(gradient_in[p], gradient_ref.at[p], sems.at[p]) for p in range(FACES)]

    @pl.loop(0, STEPS)
    def _(t):
        matrix_copy(matrix_in, matrix, matrix_sems, t).wait()
        high_ref[:, tile_at(t)], low_ref[:, tile_at(t)] = split(matrix[:, tile_at(t)])

    for copy in copies:
        copy.wait()


def ready_call(gradient, matrix):
    half = shaped(INTERFACE, INTERFACE, dtype=jnp.bfloat16)
    return call(
        ready_kernel,
        "ready",
        [shaped(FACES, MULT_ROWS, FACE_ROWS), half, half],
        4 << 20,
        8 << 20,
        [HBM] * (FACES + 1),
        scratch=MATRIX + [pltpu.SemaphoreType.DMA((FACES,))],
    )(*gradient, matrix)


def ready_last_kernel(adjoint_in, adjoint_ref, sem):
    fetched(adjoint_in, adjoint_ref, sem).wait()


def ready_last_call(adjoint):
    (out,) = call(
        ready_last_kernel,
        "ready_last",
        [shaped(FACES, COLUMNS, FACE_ROWS)],
        1 << 20,
        2 << 20,
        [HBM],
        scratch=[pltpu.SemaphoreType.DMA],
    )(adjoint)
    return out


def middle_kernel(onehot_ref, gradient_ref, high_ref, low_ref, *refs):
    near, far, adjoint_out = refs[:FACES], refs[FACES : 2 * FACES], refs[2 * FACES]
    outs = refs[2 * FACES + 1 : 3 * FACES + 1]
    sems, kept, value, rows, result = refs[3 * FACES + 1 :]
    copies = []
    for p in range(FACES):
        adjoint = near[p][...] + far[p][...]
        kept[p] = adjoint
        copies.append(fetched(kept.at[p], adjoint_out.at[p], sems.at[p]))
        put(value, face_at(p), adjoint)
    to_rows(onehot_ref, value, rows)

    @pl.loop(0, STEPS)
    def _(t):
        put(result, tile_at(t), product(rows, high_ref[:, tile_at(t)], low_ref[:, tile_at(t)]))

    for p in range(FACES):
        out = folded(mul(result[...], onehot_ref[:, face_at(p)], NN))
        outs[p][:COLUMNS] = gradient_ref[p, BODY] - out
        outs[p][COLUMNS:] = gradient_ref[p, COLUMNS:]
    for copy in copies:
        copy.wait()


def middle_call(onehot, ready, near, far):
    return call(
        middle_kernel,
        "middle",
        [in_hbm(FACES, COLUMNS, FACE_ROWS)] + [shaped(MULT_ROWS, FACE_ROWS)] * FACES,
        6 << 30,
        12 << 20,
        [VMEM] * (4 + 2 * FACES),
        scratch=[pltpu.SemaphoreType.DMA((FACES,)), FACE_BLOCK] + [PAIR] * 3,
    )(onehot, *ready, *near, *far)


def last_kernel(onehot_ref, adjoint_ref, *refs):
    near, far = refs[:FACES], refs[FACES : 2 * FACES]
    out_ref, value, staged, sems = refs[2 * FACES :]
    for p in range(FACES):
        put(value, face_at(p), adjoint_ref[p] + near[p][...] + far[p][...])
    copies = []
    for t in range(STEPS):
        at = slice(t * TILE, (t + 1) * TILE)
        out = mul(onehot_ref[at, :], value[...], NT)
        staged[t] = out[:, :COLUMNS] + out[:, COLUMNS:]
        copies.append(fetched(staged.at[t], out_ref.at[at], sems.at[t]))
    for copy in copies:
        copy.wait()


def last_call(onehot, adjoint, near, far):
    (out,) = call(
        last_kernel,
        "last",
        [in_hbm(INTERFACE, COLUMNS)],
        1 << 30,
        6 << 20,
        [VMEM] * (2 + 2 * FACES),
        scratch=[
            PAIR,
            pltpu.VMEM((STEPS, TILE, COLUMNS), jnp.float32),
            pltpu.SemaphoreType.DMA((STEPS,)),
        ],
    )(onehot, adjoint, *near, *far)
    return out


def on_device(
    objective, schur, local_inverse, coarse_basis, coarse_inverse, stiffness, face_rows, coarse_map
):
    n_grp, n_dev = lax.axis_size("grp"), lax.axis_size("dev")
    nx = X_SIZE
    nz = n_dev // nx
    grp = lax.axis_index("grp").astype(jnp.int32)
    dev = lax.axis_index("dev").astype(jnp.int32)
    x_pos = (dev % nx).reshape(1)
    z_groups = [[z * nx + x for z in range(nz)] for x in range(nx)]
    odd = jnp.stack([dev % 2, grp % 2])
    at = grp.reshape(1)

    def swap(value, axis, k):
        size = lax.axis_size(axis)
        return lax.ppermute(value, axis, [(i, i ^ k) for i in range(size)])

    def swap_next(value, axis):
        lower = range(1, lax.axis_size(axis) - 1, 2)
        return lax.ppermute(
            value, axis, [(i, i + 1) for i in lower] + [(i + 1, i) for i in lower]
        )

    def group_gather(value):
        parts = {k: swap(value, "grp", k) for k in (2, 6, 4)}
        parts = [value] + [parts[k] for k in range(2, n_grp, 2)]
        half = join_call(parts)
        return half, swap(half, "grp", 1)

    rounds = [
        lambda value: swap(value, "dev", 1),
        lambda value: swap_next(value, "dev"),
        lambda value: swap(value, "grp", 1),
        lambda value: swap_next(value, "grp"),
    ]

    def exchange(faces):
        return [turn(value) for turn, value in zip(rounds, faces)]

    local_map = coarse_map[0, 0]
    basis, onehot, *gradient = pack_call(
        odd, face_rows[0, 0], objective[0, 0], coarse_basis[0, 0], stiffness[0]
    )
    tile, *gradient = lax.optimization_barrier((coarse_inverse, *gradient))
    high, low = tile_call(tile.reshape(-1, tile.shape[3]))
    arrived = exchange(gradient)

    map_row = jnp.zeros((8, COLUMNS), jnp.float32)
    map_row = map_row.at[0, :LOCAL].set(local_map.astype(jnp.float32))
    high, low, map_row = lax.optimization_barrier((high, low, map_row))

    weighted, terms, weight, lift = weigh_call(gradient, arrived, basis, map_row, True)
    adjoint = None
    for sweep in range(SWEEPS):
        first = sweep == 0
        half, other = group_gather(terms)
        blocks = coarse_call(x_pos, half, other, high, low, n_grp, nz, nx)
        through = [swap(blocks[4], "dev", 1), swap(blocks[5], "dev", 3)]
        direct = [swap(blocks[2], "dev", 1), swap(blocks[7], "dev", 3)]
        passed = [
            swap(merge_call(blocks[6], through[0]), "dev", 3),
            swap(merge_call(blocks[3], through[1]), "dev", 1),
        ]
        total = add_call(blocks[0], direct[0], passed[0], blocks[1], passed[1], direct[1])
        total = lax.all_to_all(
            total.reshape(nz, OWNED, COLUMNS), "dev", 0, 0, axis_index_groups=z_groups, tiled=True
        )
        held, _ = lax.optimization_barrier((weighted, direct[0]))
        near = local_call(onehot, held, local_inverse[0, 0], weight)
        total, *near = lax.optimization_barrier((total, *near))
        owned = sum_call(total.reshape(nz * OWNED, COLUMNS))
        half, other = group_gather(owned)
        *near, _ = lax.optimization_barrier((*near, half))
        near = update_call(at, map_row, half, other, *bring_call(lift, near), n_grp)
        far = exchange(near)
        if first:
            matrix, _ = lax.optimization_barrier((schur, near[0]))
            ready = ready_call(gradient, matrix[0, 0])
            adjoint, *remain = middle_call(onehot, ready, near, far)
            weighted, terms = weigh_call(remain, exchange(remain), basis, map_row, False)
        else:
            kept, _ = lax.optimization_barrier((adjoint, near[0]))
            out = last_call(onehot, ready_last_call(kept), near, far)
    return out[None, None]


def solution(mesh):
    return jax.shard_map(
        on_device,
        mesh=mesh,
        in_specs=(
            P("grp", "dev", None, None),
            P("grp", "dev", None, None),
            P("grp", "dev", None, None),
            P("grp", "dev", None, None),
            P(None, "dev", None, "grp"),
            P("grp", "dev", None),
            P("grp", "dev", None, None),
            P("grp", "dev", None),
        ),
        out_specs=P("grp", "dev", None, None),
        check_vma=False,
    )
```
